256 devices in a mesh: basin: 32 (over y, x, core), tm: 8 (over z).
Axes of the slice: x: 4, y: 4, z: 8, core: 2. Of those that a mesh axis runs over, the one named last changes fastest.
Arguments:
- inflow: float32 [256, 131072], P('tm', 'basin'), may hold values from 0.01 to 0.1
- cotangent: float32 [256, 65536], P('tm', 'basin'), may hold values from -6 to 6
- gauge_reach: int32 [65536], P('basin'), may hold values from 0 to 4095
- shape_param: float32 [131072], P('basin'), may hold values from 1.5 to 4
- scale_param: float32 [131072], P('basin'), may hold values from 1.5 to 10
- block_level: int32 [512], P('basin'), may hold values from 0 to 7, as said below
- down_local: int32 [131072], P('basin'), may hold values from -1 to 4095, as said below
- in_slot: int32 [131072], P('basin'), may hold values from -1 to 127, as said below
- send_reach: int32 [32, 7, 128], P('basin'), may hold values from -1 to 4095, as said below
Outputs:
- lateral_grad: float32 [256, 131072], P('tm', 'basin')
- param_grad: float32 [2, 131072], P(None, 'basin')
The draws below stay inside these ranges and needn't reach their ends.
Inputs may be any that keep to these rules, and one draw needn't show every extreme that they name: `block_level`: every partition holds between one and 4 blocks of each level, and exactly 4 blocks of some level. `down_local`: for a reach in a block of level h >= 1 whose in_slot is -1: a reach of the same partition in a block of level h - 1. -1 for reaches of level 0 and for reaches with in_slot >= 0. `in_slot`: A value s * 4 + c (s a partition other than the reach's own, c < 4) marks a reach of level h >= 1 fed by slot c that partition s fills for it at level h - 1; within one partition no value repeats among the reaches of one level. Exactly the slots that send_reach fills are received. send_reach[s, h, t * 4 + c] is a reach of partition s in a block of level h, or -1 for an empty slot; slots with t = s are empty. At some level some partition t receives all 4 slots from every other partition.
All inputs are finite; a program needn't handle non-finite values.
Results may differ from the reference program's by a relative error of at most 0.0003.
Values sent between devices are 32-bit elements; how exact they have to be, the bound alone decides.
A program may use at most 128 MiB of HBM per device.

```python
import math
import jax
import jax.numpy as jnp

BLK = 256
BDEV = 16
LAGS = 30
LEVELS = 8
CAP = 4
MAXB = 4
REACHES = 131072
DAYS = 256
GAUGES = 65536
N_BASIN = 32


def topology(key):
    parts = N_BASIN
    per_device = BDEV * BLK
    keys = [jax.random.fold_in(key, 7000 + number) for number in range(12)]
    heavy = jax.random.randint(keys[0], (parts,), 0, LEVELS)
    offset = jax.random.randint(keys[1], (parts,), 0, LEVELS - 1)
    place = jnp.arange(BDEV, dtype=jnp.int32)[None, :]
    spread = jnp.where(place < MAXB + LEVELS - 1, place - MAXB, place - MAXB - LEVELS + 1 + offset[:, None]) % (LEVELS - 1)
    other = spread + (spread >= heavy[:, None]).astype(jnp.int32)
    base_level = jnp.where(place < MAXB, heavy[:, None], other)
    orders = jax.vmap(lambda sub: jax.random.permutation(sub, BDEV))(jax.random.split(keys[2], parts))
    levels = jnp.take_along_axis(base_level, orders, axis=1).astype(jnp.int32)
    level_ids = jnp.arange(LEVELS, dtype=jnp.int32)
    onehot = (levels[:, :, None] == level_ids[None, None, :]).astype(jnp.int32)
    counts = jnp.sum(onehot, axis=1)
    rank_own = jnp.sum((jnp.cumsum(onehot, axis=1) - 1) * onehot, axis=2)
    slot_ids = jnp.arange(MAXB, dtype=jnp.int32)
    block_ids = jnp.arange(BDEV, dtype=jnp.int32)
    matches = (levels[:, None, None, :] == level_ids[None, :, None, None]) & (rank_own[:, None, None, :] == slot_ids[None, None, :, None])
    table = jnp.sum(jnp.where(matches, block_ids[None, None, None, :], 0), axis=3)
    dev_grid = jnp.arange(parts, dtype=jnp.int32)[:, None, None]
    reach_level = jnp.broadcast_to(levels[:, :, None], (parts, BDEV, BLK))
    lower = jnp.maximum(reach_level - 1, 0)
    pick = jax.random.randint(keys[3], (parts, BDEV, BLK), 0, counts[dev_grid, lower])
    down_block = table[dev_grid, lower, pick]
    down_pos = jax.random.randint(keys[4], (parts, BDEV, BLK), 0, BLK)
    down = jnp.where(reach_level >= 1, down_block * BLK + down_pos, -1).reshape(parts * per_device)
    shape = (parts, LEVELS - 1, parts, CAP)
    src = jnp.arange(parts, dtype=jnp.int32)[:, None, None, None]
    lev = jnp.arange(LEVELS - 1, dtype=jnp.int32)[None, :, None, None]
    dst = jnp.arange(parts, dtype=jnp.int32)[None, None, :, None]
    cap_ids = jnp.arange(CAP, dtype=jnp.int32)[None, None, None, :]
    coin = jax.random.randint(keys[5], shape, 0, 2) == 1
    full_dst = jax.random.randint(keys[6], (), 0, parts)
    full_lev = jax.random.randint(keys[7], (), 0, LEVELS - 1)
    filled = (coin | (dst == full_dst) & (lev == full_lev)) & (src != dst)
    send_pick = jax.random.randint(keys[8], shape, 0, counts[src, lev])
    send_block = table[src, lev, send_pick]
    send_pos = jax.random.randint(keys[9], shape, 0, BLK)
    sends = jnp.where(filled, send_block * BLK + send_pos, -1).reshape(parts, LEVELS - 1, parts * CAP)
    recv_pick = jax.random.randint(keys[10], shape, 0, counts[dst, lev + 1])
    recv_block = table[dst, lev + 1, recv_pick]
    perm_keys = jax.random.split(keys[11], parts * (LEVELS - 1))
    perms = jax.vmap(lambda sub: jax.random.permutation(sub, BLK))(perm_keys).reshape(parts, LEVELS - 1, BLK).astype(jnp.int32)
    slot_value = src * CAP + cap_ids + 0 * lev + 0 * dst
    recv_pos = perms[dst, lev, slot_value]
    target = jnp.where(filled, dst * per_device + recv_block * BLK + recv_pos, parts * per_device)
    slots = jnp.full((parts * per_device,), -1, jnp.int32).at[target.reshape(-1)].set(slot_value.reshape(-1), mode='drop')
    down = jnp.where(slots >= 0, -1, down).astype(jnp.int32)
    return (levels.reshape(parts * BDEV), down, slots, sends.astype(jnp.int32))


def draw_block_level(key, part):
    return topology(key)[0]


def draw_down_local(key, part):
    return topology(key)[1]


def draw_in_slot(key, part):
    return topology(key)[2]


def draw_send_reach(key, part):
    return topology(key)[3]


def touch_ends(result, rng, least, largest):
    spot = [jax.random.randint(jax.random.fold_in(rng, axis), (), 0, length) for axis, length in enumerate(result.shape)]
    widest = result.shape.index(max(result.shape))
    neighbour = spot[:widest] + [(spot[widest] + 1) % result.shape[widest]] + spot[widest + 1:]
    return result.at[tuple(spot)].set(least).at[tuple(neighbour)].set(largest)


def shard_levels(own_key, extent, shards, smallest, largest):
    def one(dim, shards_of):
        draws = jax.random.uniform(jax.random.fold_in(jax.random.fold_in(own_key, 6), dim), (shards_of,), jnp.float32, smallest / len(shards), largest / len(shards))
        return jnp.repeat(jnp.exp(draws), extent[dim] // shards_of).reshape((-1,) + (1,) * (len(extent) - dim - 1))

    loudness = one(*shards[0])
    for cut in shards[1:]:
        loudness = loudness * one(*cut)
    return loudness


def centred(own_key, shape, width, reach, shards=(), held_as=jnp.bfloat16):
    drawn = width * jax.random.normal(own_key, shape, jnp.float32)
    if shards:
        drawn = drawn * shard_levels(own_key, shape, shards, -0.22, 0.18)
    return jnp.clip(drawn, -reach, reach).astype(held_as)


def setup_inputs(seed: int = 0) -> dict:
    splits = jax.random.split(jax.random.key(seed), 10)
    inflow = jnp.clip(jnp.exp(math.log(0.1) - 2.3025851 * jax.random.uniform(splits[0], (DAYS, REACHES), jnp.float32) ** shard_levels(splits[0], (DAYS, REACHES), ((0, 8), (1, 32)), -0.2, 0.2)), 0.01, 0.1)
    cotangent = centred(splits[1], (DAYS, GAUGES), 1.0, 6.0, ((0, 8), (1, 32)), jnp.float32)
    gauge_reach = touch_ends(jax.random.randint(splits[2], (GAUGES,), 0, BDEV * BLK), jax.random.fold_in(splits[2], 1), 0, (BDEV * BLK) - 1).astype(jnp.int32)
    shape_param = jnp.clip(1.5 + 2.5 * jax.random.uniform(splits[3], (REACHES,), jnp.float32) ** shard_levels(splits[3], (REACHES,), ((0, 32),), -0.2, 0.2), 1.5, 4.0)
    scale_param = jnp.clip(jnp.exp(math.log(10.0) - 1.89712 * jax.random.uniform(splits[4], (REACHES,), jnp.float32) ** shard_levels(splits[4], (REACHES,), ((0, 32),), -0.2, 0.2)), 1.5, 10.0)
    block_level = draw_block_level(jax.random.fold_in(splits[9], 71), 0)
    down_local = draw_down_local(jax.random.fold_in(splits[9], 71), 0)
    in_slot = draw_in_slot(jax.random.fold_in(splits[9], 71), 0)
    send_reach = draw_send_reach(jax.random.fold_in(splits[9], 71), 0)
    return {"inflow": inflow, "cotangent": cotangent, "gauge_reach": gauge_reach, "shape_param": shape_param, "scale_param": scale_param, "block_level": block_level, "down_local": down_local, "in_slot": in_slot, "send_reach": send_reach}


def kernel_of(shape_param, scale_param, lag_count):
    offsets = jnp.arange(lag_count, dtype=jnp.float32) + 0.5
    logits = (shape_param[None, :] - 1.0) * jnp.log(offsets)[:, None] - offsets[:, None] / scale_param[None, :]
    weights = jnp.exp(logits)
    return weights / jnp.sum(weights, axis=0, keepdims=True), offsets


def lag_adjoint(kernel, extended, day_count):
    summed = kernel[0][None, :] * extended[0:day_count]
    for lag_index in range(1, kernel.shape[0]):
        summed = summed + kernel[lag_index][None, :] * extended[lag_index:lag_index + day_count]
    return summed


def lag_gradient(adjoint_in, inflow_ext, lag_count, day_count):
    per_lag = []
    for lag_index in range(lag_count):
        first_day = lag_count - 1 - lag_index
        per_lag.append(jnp.sum(adjoint_in * inflow_ext[first_day:first_day + day_count], axis=0))
    return jnp.stack(per_lag)


def param_terms(kernel, offsets, scale_param, kernel_grad):
    weighted = jnp.sum(kernel * kernel_grad, axis=0, keepdims=True)
    logit_grad = kernel * (kernel_grad - weighted)
    shape_grad = jnp.sum(logit_grad * jnp.log(offsets)[:, None], axis=0)
    scale_grad = jnp.sum(logit_grad * offsets[:, None], axis=0) / (scale_param * scale_param)
    return jnp.stack([shape_grad, scale_grad])


def reference(inflow, cotangent, gauge_reach, shape_param, scale_param, block_level, down_local, in_slot, send_reach):
    day_count = inflow.shape[0]
    lag_count = LAGS
    per_device = BDEV * BLK
    kernel, offsets = kernel_of(shape_param, scale_param, lag_count)
    owners = (jnp.arange(GAUGES, dtype=jnp.int32) // (GAUGES // N_BASIN)) * per_device + gauge_reach
    gauge_seed = jnp.zeros((day_count, REACHES), jnp.float32).at[:, owners].add(cotangent)
    inflow_ext = jnp.concatenate([jnp.zeros((lag_count - 1, REACHES), jnp.float32), inflow], axis=0)
    device_base = jnp.arange(N_BASIN, dtype=jnp.int32) * per_device
    positions = jnp.arange(BLK, dtype=jnp.int32)
    slot_ids = jnp.arange(MAXB, dtype=jnp.int32)
    block_ids = jnp.arange(BDEV, dtype=jnp.int32)
    level_grid = block_level.reshape(N_BASIN, BDEV)
    owner_dev = jnp.repeat(jnp.arange(N_BASIN, dtype=jnp.int32), MAXB * BLK)
    adjoint_all = jnp.zeros((day_count, REACHES), jnp.float32)
    kernel_grad = jnp.zeros((lag_count, REACHES), jnp.float32)
    received = jnp.zeros((day_count, N_BASIN, N_BASIN * CAP), jnp.float32)
    for height in range(LEVELS):
        at_height = level_grid == height
        rank_of = jnp.cumsum(at_height.astype(jnp.int32), axis=1) - 1
        slot_hits = at_height[:, None, :] & (rank_of[:, None, :] == slot_ids[None, :, None])
        slot_valid = jnp.any(slot_hits, axis=2)
        chosen = jnp.sum(jnp.where(slot_hits, block_ids[None, None, :], 0), axis=2)
        local_cols = (chosen[:, :, None] * BLK + positions[None, None, :]).reshape(N_BASIN, MAXB * BLK)
        columns = (local_cols + device_base[:, None]).reshape(-1)
        below_reach = down_local[columns]
        local_part = jnp.where(below_reach[None, :] >= 0, adjoint_all[:, owner_dev * per_device + jnp.maximum(below_reach, 0)], 0.0)
        slot_of = in_slot[columns]
        remote_part = jnp.where(slot_of[None, :] >= 0, received[:, owner_dev, jnp.maximum(slot_of, 0)], 0.0)
        adjoint_in = gauge_seed[:, columns] + local_part + remote_part
        extended = jnp.concatenate([adjoint_in, jnp.zeros((lag_count - 1, adjoint_in.shape[1]), jnp.float32)], axis=0)
        outflow = lag_adjoint(kernel[:, columns], extended, day_count)
        lag_grads = lag_gradient(adjoint_in, inflow_ext[:, columns], lag_count, day_count)
        targets = jnp.where(jnp.repeat(slot_valid.reshape(-1), BLK), columns, REACHES)
        adjoint_all = adjoint_all.at[:, targets].set(outflow, mode="drop")
        kernel_grad = kernel_grad.at[:, targets].set(lag_grads, mode="drop")
        if height + 1 < LEVELS:
            wanted = send_reach[:, height, :]
            outgoing = jnp.where(wanted[None, :, :] >= 0, adjoint_all[:, device_base[:, None] + jnp.maximum(wanted, 0)], 0.0)
            received = outgoing.reshape(day_count, N_BASIN, N_BASIN, CAP).transpose(0, 2, 1, 3).reshape(day_count, N_BASIN, N_BASIN * CAP)
    param_grad = param_terms(kernel, offsets, scale_param, kernel_grad)
    return adjoint_all, param_grad
```

```python
import functools
import math

import jax
import jax.numpy as jnp
from jax import lax
from jax.experimental import pallas as pl
from jax.experimental.pallas import tpu as pltpu
from jax.sharding import PartitionSpec as P

BLK = 256
LAGS = 30
LEVELS = 8
MAXB = 4
CAP = 4
LANES = 128
TILES = MAXB * BLK // LANES
HALO = LAGS - 1
OFFSETS = [k + 0.5 for k in range(LAGS)]
LOGS = [math.log(o) for o in OFFSETS]


def block_tables(block_level):
    ids = jnp.arange(block_level.shape[0], dtype=jnp.int32)
    before = (block_level[None, :] == block_level[:, None]) & (ids[None, :] < ids[:, None])
    place = block_level * MAXB + jnp.sum(before.astype(jnp.int32), axis=1)
    slots = jnp.arange(LEVELS * MAXB, dtype=jnp.int32)
    order = jnp.sum(jnp.where(place[None, :] == slots[:, None], ids[None, :], 0), axis=1)
    return jnp.concatenate([order, place])


def adjoint_kernel(
    parts,
    shifts,
    days,
    table,
    cot,
    gauge,
    inflow,
    shape_p,
    scale_p,
    down,
    inslot,
    send,
    lat,
    par,
    cot2,
    gpos,
    seed,
    infl,
    kern,
    dlane,
    dtile,
    rlane,
    wlane,
    wtile,
    scl_lv,
    adj,
    lday,
    xsend,
    xrecv,
    out_msg,
    own_msg,
    far_msg,
    turn,
    rows_own,
    rows_far,
    lag_sum,
    psend,
    precv,
    ptotal,
    lat_lv,
    staged,
    sx,
    rx,
    so,
    sf,
    ro,
    rf,
    sp,
    rp,
):
    blocks = inflow.shape[1] // BLK
    me = lax.axis_index("basin")
    shift = lax.axis_index("tm")
    prev = lax.rem(shift + shifts - 1, shifts)
    has_next = shift < shifts - 1

    def tile_of(reach):
        block = reach >> 8
        slot = jnp.zeros_like(reach)
        for b in range(blocks):
            slot = jnp.where(block == b, table[LEVELS * MAXB + b], slot)
        return slot, (slot & (MAXB - 1)) * 2 + ((reach >> 7) & 1)

    def prepare(h):
        spots = [table[h * MAXB + m] * 2 + j for m in range(MAXB) for j in range(2)]

        def tiled(ref):
            return jnp.concatenate([ref[pl.ds(i, 1), :] for i in spots], axis=0)

        target = tiled(down)
        dtile[h] = jnp.where(target >= 0, tile_of(target)[1], -1)
        dlane[h] = target & (LANES - 1)
        rlane[h] = tiled(inslot)
        shp = tiled(shape_p) - 1.0
        scl = tiled(scale_p)
        scl_lv[h] = scl
        weights = [jnp.exp(shp * LOGS[k] - OFFSETS[k] / scl) for k in range(LAGS)]
        total = weights[0]
        for k in range(1, LAGS):
            total = total + weights[k]
        for k in range(LAGS):
            kern[h, k] = weights[k] / total

    def seeds(h):
        width = 2 * LANES
        local = gpos[...] - h * (MAXB * BLK)

        ids = lax.broadcasted_iota(jnp.int32, (width, local.shape[1]), 0)
        for c in range(MAXB * BLK // width):
            hot = jnp.where(ids == local - c * width, 1.0, 0.0).astype(jnp.bfloat16)
            both = lax.dot_general(
                cot2[...], hot, (((1,), (1,)), ((), ())), preferred_element_type=jnp.float32
            )
            sums = both[:days] + both[days:]
            for j in range(width // LANES):
                seed[h, :, 2 * c + j, :] = sums[:, j * LANES : (j + 1) * LANES]

    def routed(h):
        total = kern[h, 0][None] * adj[pl.ds(0, days)]
        for k in range(1, LAGS):
            total = total + kern[h, k][None] * adj[pl.ds(k, days)]
        lday[...] = total

    def outgoing(h):
        lane, tile = wlane[h], wtile[h]
        for g in range(days // 8):
            picked = jnp.zeros((8, LANES), jnp.float32)
            for s in range(TILES):
                got = jnp.take_along_axis(lday[pl.ds(8 * g, 8), s, :], lane, axis=1)
                picked = jnp.where(tile == s, got, picked)
            turn[0, 8 * g : 8 * g + 8, :] = picked
        turn[0] = jnp.transpose(turn[0])
        lanes = lax.broadcasted_iota(jnp.int32, (parts, LANES), 1)
        packed = jnp.zeros((parts, LANES), jnp.float32)
        for c in range(CAP):
            piece = turn[0, pl.ds(c, parts, stride=CAP), :]
            piece = pltpu.roll(piece, c * days, axis=1) if c else piece
            packed = jnp.where((lanes >= c * days) & (lanes < (c + 1) * days), piece, packed)
        out_msg[h, :, 0, :] = packed

    def slot_copy(h, q, target, ssem, buf, rsem):
        return pltpu.make_async_remote_copy(
            src_ref=out_msg.at[h, q],
            dst_ref=buf.at[h, me],
            send_sem=ssem.at[h],
            recv_sem=rsem.at[h],
            device_id={"basin": q, "tm": target},
            device_id_type=pl.DeviceIdType.MESH,
        )

    def send_slots(h):
        @pl.loop(1, parts)
        def _(i):
            q = lax.rem(me + i, parts)
            slot_copy(h, q, prev, sf, far_msg, rf).start()
            slot_copy(h, q, shift, so, own_msg, ro).start()

    def local_part(h):
        lane, tile = dlane[h], dtile[h]
        masks = [tile == s for s in range(TILES)]

        @pl.loop(0, days, unroll=4)
        def _(t):
            got = jnp.zeros((TILES, LANES), jnp.float32)
            for s in range(TILES):
                line = jnp.broadcast_to(lday[t, s : s + 1, :], (TILES, LANES))
                got = jnp.where(masks[s], jnp.take_along_axis(line, lane, axis=1), got)
            xsend[h, t] = seed[h, t] + got

    def halo_copy(h):
        return pltpu.make_async_remote_copy(
            src_ref=xsend.at[h, pl.ds(0, HALO)],
            dst_ref=xrecv.at[h],
            send_sem=sx.at[h],
            recv_sem=rx.at[h],
            device_id={"basin": me, "tm": prev},
            device_id_type=pl.DeviceIdType.MESH,
        )

    def unpack(h, buf, rows):
        arrived = buf[h, :, 0, :]
        for c in range(CAP):
            piece = pltpu.roll(arrived, LANES - c * days, axis=1) if c else arrived
            turn[1, pl.ds(c, parts, stride=CAP), :] = piece
        rows[...] = jnp.transpose(turn[1])[: rows.shape[0]]

    def remote_part(h, row):
        slot = rlane[h]
        line = jnp.broadcast_to(row, (TILES, LANES))
        got = jnp.take_along_axis(line, slot & (LANES - 1), axis=1)
        return jnp.where(slot >= 0, got, 0.0)

    def gradient(h):
        for m in range(MAXB):
            block = table[h * MAXB + m]
            for j in range(2):
                infl[:, 2 * m + j, :] = staged[block * 2 + j]
        for k in range(LAGS):
            lag_sum[k] = jnp.sum(infl[...] * adj[pl.ds(k, days)], axis=0)
        mean = kern[h, 0] * lag_sum[0]
        for k in range(1, LAGS):
            mean = mean + kern[h, k] * lag_sum[k]
        first = jnp.zeros((TILES, LANES), jnp.float32)
        second = jnp.zeros((TILES, LANES), jnp.float32)
        for k in range(LAGS):
            logit = kern[h, k] * (lag_sum[k] - mean)
            first = first + logit * LOGS[k]
            second = second + logit * OFFSETS[k]
        scl = scl_lv[h]
        psend[h, 0] = first
        psend[h, 1] = second / (scl * scl)

    def grad_copy(h, i):
        return pltpu.make_async_remote_copy(
            src_ref=psend.at[h],
            dst_ref=precv.at[h, i - 1],
            send_sem=sp.at[h],
            recv_sem=rp.at[h],
            device_id={"basin": me, "tm": lax.rem(shift + i, shifts)},
            device_id_type=pl.DeviceIdType.MESH,
        )

    def send_grads(h):
        for i in range(1, shifts):
            grad_copy(h, i).start()

    def keep(h):
        for s in range(TILES):
            lat_lv[h * TILES + s] = lday[:, s, :]

    def wait_bytes(ref, sem):
        pltpu.make_async_copy(ref, ref, sem).wait()

    value = cot[...]
    high = value.astype(jnp.bfloat16)
    cot2[pl.ds(0, days), :] = high
    cot2[pl.ds(days, days), :] = (value - high.astype(jnp.float32)).astype(jnp.bfloat16)
    reach = gauge[...]
    gpos[...] = tile_of(reach)[0] * BLK + (reach & (BLK - 1))
    seeds(0)
    xsend[0] = seed[0]
    halo_copy(0).start()
    wanted = jnp.maximum(send[...], 0)
    wanted_tile = tile_of(wanted)[1]
    for h in range(LEVELS - 1):
        wlane[h] = jnp.broadcast_to(wanted[h : h + 1, :] & (LANES - 1), (8, LANES))
        wtile[h] = jnp.broadcast_to(wanted_tile[h : h + 1, :], (8, LANES))
    turn[...] = jnp.zeros_like(turn)
    for i in range(2 * blocks):
        staged[i] = inflow[:, i * LANES : (i + 1) * LANES]
    prepare(0)
    prepare(1)
    seeds(1)
    halo_copy(0).wait_recv()
    adj[pl.ds(0, days)] = xsend[0]
    adj[pl.ds(days, HALO)] = jnp.where(has_next, xrecv[0], 0.0)

    @pl.loop(0, LEVELS - 1)
    def _(h):
        routed(h)
        outgoing(h)
        send_slots(h)
        local_part(h + 1)
        halo_copy(h + 1).start()
        gradient(h)
        send_grads(h)
        keep(h)

        @pl.when(h < LEVELS - 2)
        def _():
            seeds(h + 2)

        prepare(jnp.minimum(h + 2, LEVELS - 1))
        wait_bytes(own_msg.at[h, pl.ds(0, parts - 1)], ro.at[h])
        unpack(h, own_msg, rows_own)
        for t in range(days):
            adj[t] = xsend[h + 1, t] + remote_part(h + 1, rows_own[t : t + 1, :])
        wait_bytes(far_msg.at[h, pl.ds(0, parts - 1)], rf.at[h])
        unpack(h, far_msg, rows_far)
        halo_copy(h + 1).wait_recv()
        for t in range(HALO):
            value = xrecv[h + 1, t] + remote_part(h + 1, rows_far[t : t + 1, :])
            adj[days + t] = jnp.where(has_next, value, 0.0)

    last = LEVELS - 1
    gradient(last)
    send_grads(last)
    routed(last)
    keep(last)
    for b in range(blocks):
        place = table[LEVELS * MAXB + b]
        for j in range(2):
            lat[:, pl.ds(b * BLK + j * LANES, LANES)] = lat_lv[place * 2 + j]

    @pl.loop(0, LEVELS)
    def _(h):
        wait_bytes(precv.at[h], rp.at[h])
        total = psend[h]
        for i in range(shifts - 1):
            total = total + precv[h, i]
        for r in range(2):
            ptotal[r, pl.ds(pl.multiple_of(h * TILES, TILES), TILES), :] = total[r]

    for b in range(blocks):
        place = table[LEVELS * MAXB + b]
        for j in range(2):
            for r in range(2):
                line = ptotal[r, pl.ds(place * 2 + j, 1), :]
                par[r : r + 1, pl.ds(b * BLK + j * LANES, LANES)] = line

    @pl.loop(0, LEVELS)
    def _(h):
        wait_bytes(xsend.at[h, pl.ds(0, HALO)], sx.at[h])
        wait_bytes(precv.at[h], sp.at[h])

    @pl.loop(0, LEVELS - 1)
    def _(h):
        wait_bytes(out_msg.at[h, pl.ds(0, parts - 1)], so.at[h])
        wait_bytes(out_msg.at[h, pl.ds(0, parts - 1)], sf.at[h])


def shards(parts, shifts, inflow, cotangent, gauge_reach, shape_param, scale_param, block_level, down_local, in_slot, send_reach):
    days, reaches = inflow.shape
    gauges = cotangent.shape[1]
    lines = reaches // LANES
    send = send_reach[0]
    if send.shape[1] < LANES:
        send = jnp.pad(send, ((0, 0), (0, LANES - send.shape[1])))
    f32, i32 = jnp.float32, jnp.int32
    levels = LEVELS
    rounds = LEVELS - 1
    tile = (TILES, LANES)
    vmem = pl.BlockSpec(memory_space=pltpu.VMEM)
    dma = pltpu.SemaphoreType.DMA
    return pl.pallas_call(
        functools.partial(adjoint_kernel, parts, shifts, days),
        out_shape=(
            jax.ShapeDtypeStruct((days, reaches), f32),
            jax.ShapeDtypeStruct((2, reaches), f32),
        ),
        in_specs=[pl.BlockSpec(memory_space=pltpu.SMEM)] + [vmem] * 8,
        out_specs=(vmem, vmem),
        scratch_shapes=[
            pltpu.VMEM((2 * days, gauges), jnp.bfloat16),
            pltpu.VMEM((1, gauges), i32),
            pltpu.VMEM((levels, days) + tile, f32),
            pltpu.VMEM((days,) + tile, f32),
            pltpu.VMEM((levels, LAGS) + tile, f32),
            pltpu.VMEM((levels,) + tile, i32),
            pltpu.VMEM((levels,) + tile, i32),
            pltpu.VMEM((levels,) + tile, i32),
            pltpu.VMEM((rounds,) + tile, i32),
            pltpu.VMEM((rounds,) + tile, i32),
            pltpu.VMEM((levels,) + tile, f32),
            pltpu.VMEM((days + HALO,) + tile, f32),
            pltpu.VMEM((days,) + tile, f32),
            pltpu.VMEM((levels, days) + tile, f32),
            pltpu.VMEM((levels, HALO) + tile, f32),
            pltpu.VMEM((rounds, parts, 1, LANES), f32),
            pltpu.VMEM((rounds, parts, 1, LANES), f32),
            pltpu.VMEM((rounds, parts, 1, LANES), f32),
            pltpu.VMEM((2, LANES, LANES), f32),
            pltpu.VMEM((days, LANES), f32),
            pltpu.VMEM((days, LANES), f32),
            pltpu.VMEM((LAGS,) + tile, f32),
            pltpu.VMEM((levels, 2) + tile, f32),
            pltpu.VMEM((levels, shifts - 1, 2) + tile, f32),
            pltpu.VMEM((2, levels * TILES, LANES), f32),
            pltpu.VMEM((levels * TILES, days, LANES), f32),
            pltpu.VMEM((lines, days, LANES), f32),
            dma((levels,)),
            dma((levels,)),
            dma((rounds,)),
            dma((rounds,)),
            dma((rounds,)),
            dma((rounds,)),
            dma((levels,)),
            dma((levels,)),
        ],
        compiler_params=pltpu.CompilerParams(
            has_side_effects=True, vmem_limit_bytes=40 * 1024 * 1024
        ),
    )(
        block_tables(block_level),
        cotangent,
        gauge_reach.reshape(1, gauges),
        inflow,
        shape_param.reshape(lines, LANES),
        scale_param.reshape(lines, LANES),
        down_local.reshape(lines, LANES),
        in_slot.reshape(lines, LANES),
        send,
    )


def solution(mesh):
    in_specs = (
        P("tm", "basin"),
        P("tm", "basin"),
        P("basin"),
        P("basin"),
        P("basin"),
        P("basin"),
        P("basin"),
        P("basin"),
        P("basin", None, None),
    )
    out_specs = (P("tm", "basin"), P(None, "basin"))
    body = functools.partial(shards, mesh.shape["basin"], mesh.shape["tm"])
    return jax.shard_map(body, mesh=mesh, in_specs=in_specs, out_specs=out_specs, check_vma=False)
```

```python
import functools
import math

import jax
import jax.numpy as jnp
from jax import lax
from jax.experimental import pallas as pl
from jax.experimental.pallas import tpu as pltpu
from jax.sharding import PartitionSpec as P

BLK = 256
LAGS = 30
LEVELS = 8
MAXB = 4
CAP = 4
LANES = 128
TILES = MAXB * BLK // LANES
HALO = LAGS - 1
UNROLL = 32
OFFSETS = [k + 0.5 for k in range(LAGS)]
LOGS = [math.log(o) for o in OFFSETS]


def adjoint_kernel(
    parts,
    shifts,
    days,
    levels,
    cot_h,
    gauge_h,
    inflow_h,
    shape_h,
    scale_h,
    down_h,
    inslot_h,
    send_h,
    lat,
    par,
    table,
    cot,
    gauge,
    shape_p,
    scale_p,
    down,
    inslot,
    send,
    load_sem,
    cot2,
    gpos,
    seed,
    infl,
    kern,
    dlane,
    dtile,
    rlane,
    wlane,
    wtile,
    scl_lv,
    adj,
    lday,
    xsend,
    xrecv,
    out_msg,
    own_msg,
    far_msg,
    turn,
    rows_own,
    rows_far,
    lag_sum,
    psend,
    precv,
    ptotal,
    lat_lv,
    staged,
    sx,
    rx,
    so,
    sf,
    ro,
    rf,
    sp,
    rp,
):
    blocks = levels.shape[0]
    me = lax.axis_index("basin")
    shift = lax.axis_index("tm")
    prev = lax.rem(shift + shifts - 1, shifts)
    has_next = shift < shifts - 1
    has_prev = shift > 0

    def tile_of(reach):
        block = reach >> 8
        slot = jnp.zeros_like(reach)
        for b in range(blocks):
            slot = jnp.where(block == b, table[LEVELS * MAXB + b], slot)
        return slot, (slot & (MAXB - 1)) * 2 + ((reach >> 7) & 1)

    def prepare(h):
        spots = [table[h * MAXB + m] * 2 + j for m in range(MAXB) for j in range(2)]

        def tiled(ref):
            return jnp.concatenate([ref[pl.ds(i, 1), :] for i in spots], axis=0)

        target = tiled(down)
        dtile[h] = jnp.where(target >= 0, tile_of(target)[1], -1)
        dlane[h] = target & (LANES - 1)
        rlane[h] = tiled(inslot)
        shp = tiled(shape_p) - 1.0
        scl = tiled(scale_p)
        scl_lv[h] = scl
        weights = [jnp.exp(shp * LOGS[k] - OFFSETS[k] / scl) for k in range(LAGS)]
        total = weights[0]
        for k in range(1, LAGS):
            total = total + weights[k]
        for k in range(LAGS):
            kern[h, k] = weights[k] / total

    def seeds(h):
        width = 2 * LANES
        local = gpos[...] - h * (MAXB * BLK)

        ids = lax.broadcasted_iota(jnp.int32, (width, local.shape[1]), 0)
        for c in range(MAXB * BLK // width):
            hot = jnp.where(ids == local - c * width, 1.0, 0.0).astype(jnp.bfloat16)
            both = lax.dot_general(
                cot2[...], hot, (((1,), (1,)), ((), ())), preferred_element_type=jnp.float32
            )
            sums = both[:days] + both[days:]
            for j in range(width // LANES):
                seed[h, :, 2 * c + j, :] = sums[:, j * LANES : (j + 1) * LANES]

    def routed(h):
        total = kern[h, 0][None] * adj[pl.ds(0, days)]
        for k in range(1, LAGS):
            total = total + kern[h, k][None] * adj[pl.ds(k, days)]
        lday[...] = total

    def outgoing(h):
        lane, tile = wlane[h], wtile[h]
        for g in range(days // 8):
            picked = jnp.zeros((8, LANES), jnp.float32)
            for s in range(TILES):
                got = jnp.take_along_axis(lday[pl.ds(8 * g, 8), s, :], lane, axis=1)
                picked = jnp.where(tile == s, got, picked)
            turn[0, 8 * g : 8 * g + 8, :] = picked
        turn[0] = jnp.transpose(turn[0])
        lanes = lax.broadcasted_iota(jnp.int32, (parts, LANES), 1)
        packed = jnp.zeros((parts, LANES), jnp.float32)
        for c in range(CAP):
            piece = turn[0, pl.ds(c, parts, stride=CAP), :]
            piece = pltpu.roll(piece, c * days, axis=1) if c else piece
            packed = jnp.where((lanes >= c * days) & (lanes < (c + 1) * days), piece, packed)
        out_msg[h, :, 0, :] = packed

    def slot_copy(h, q, target, ssem, buf, rsem):
        return pltpu.make_async_remote_copy(
            src_ref=out_msg.at[h, q],
            dst_ref=buf.at[h, me],
            send_sem=ssem.at[h],
            recv_sem=rsem.at[h],
            device_id={"basin": q, "tm": target},
            device_id_type=pl.DeviceIdType.MESH,
        )

    def send_slots(h):
        @pl.loop(1, parts)
        def _(i):
            q = lax.rem(me + i, parts)
            slot_copy(h, q, shift, so, own_msg, ro).start()

        @pl.when(has_prev)
        def _():
            @pl.loop(1, parts)
            def _(i):
                q = lax.rem(me + i, parts)
                slot_copy(h, q, prev, sf, far_msg, rf).start()

    def local_part(h):
        lane, tile = dlane[h], dtile[h]
        masks = [tile == s for s in range(TILES)]

        @pl.loop(0, days, unroll=UNROLL)
        def _(t):
            got = jnp.zeros((TILES, LANES), jnp.float32)
            for s in range(TILES):
                line = jnp.broadcast_to(lday[t, s : s + 1, :], (TILES, LANES))
                got = jnp.where(masks[s], jnp.take_along_axis(line, lane, axis=1), got)
            xsend[h, t] = seed[h, t] + got

    def halo_copy(h):
        return pltpu.make_async_remote_copy(
            src_ref=xsend.at[h, pl.ds(0, HALO)],
            dst_ref=xrecv.at[h],
            send_sem=sx.at[h],
            recv_sem=rx.at[h],
            device_id={"basin": me, "tm": prev},
            device_id_type=pl.DeviceIdType.MESH,
        )

    def send_halo(h):
        @pl.when(has_prev)
        def _():
            halo_copy(h).start()

    def take_halo(h):
        @pl.when(has_next)
        def _():
            halo_copy(h).wait_recv()

    def unpack(h, buf, rows):
        arrived = buf[h, :, 0, :]
        for c in range(CAP):
            piece = pltpu.roll(arrived, LANES - c * days, axis=1) if c else arrived
            turn[1, pl.ds(c, parts, stride=CAP), :] = piece
        rows[...] = jnp.transpose(turn[1])[: rows.shape[0]]

    def remote_part(h, row):
        slot = rlane[h]
        line = jnp.broadcast_to(row, (TILES, LANES))
        got = jnp.take_along_axis(line, slot & (LANES - 1), axis=1)
        return jnp.where(slot >= 0, got, 0.0)

    def gradient(h):
        for m in range(MAXB):
            block = table[h * MAXB + m]
            for j in range(2):
                infl[:, 2 * m + j, :] = staged[block * 2 + j]
        for k in range(LAGS):
            lag_sum[k] = jnp.sum(infl[...] * adj[pl.ds(k, days)], axis=0)
        mean = kern[h, 0] * lag_sum[0]
        for k in range(1, LAGS):
            mean = mean + kern[h, k] * lag_sum[k]
        first = jnp.zeros((TILES, LANES), jnp.float32)
        second = jnp.zeros((TILES, LANES), jnp.float32)
        for k in range(LAGS):
            logit = kern[h, k] * (lag_sum[k] - mean)
            first = first + logit * LOGS[k]
            second = second + logit * OFFSETS[k]
        scl = scl_lv[h]
        psend[h, 0] = first
        psend[h, 1] = second / (scl * scl)

    def grad_copy(h, i):
        return pltpu.make_async_remote_copy(
            src_ref=psend.at[h],
            dst_ref=precv.at[h, i - 1],
            send_sem=sp.at[h],
            recv_sem=rp.at[h],
            device_id={"basin": me, "tm": lax.rem(shift + i, shifts)},
            device_id_type=pl.DeviceIdType.MESH,
        )

    def send_grads(h):
        for i in range(1, shifts):
            grad_copy(h, i).start()

    def keep(h):
        for s in range(TILES):
            lat_lv[h * TILES + s] = lday[:, s, :]

    def wait_bytes(ref, sem):
        pltpu.make_async_copy(ref, ref, sem).wait()

    barrier = pltpu.get_barrier_semaphore()

    def greet(q, k):
        where = {"basin": q, "tm": k}
        pl.semaphore_signal(barrier, inc=1, device_id=where, device_id_type=pl.DeviceIdType.MESH)

    loads = [
        pltpu.make_async_copy(src, dst, load_sem.at[i])
        for i, (src, dst) in enumerate(
            [(cot_h, cot), (gauge_h, gauge), (shape_h, shape_p), (scale_h, scale_p), (down_h, down), (inslot_h, inslot), (send_h, send)]
        )
    ]
    for copy in loads:
        copy.start()
    for i in range(2 * blocks):
        pltpu.make_async_copy(
            inflow_h.at[:, pl.ds(i * LANES, LANES)], staged.at[i], load_sem.at[len(loads)]
        ).start()

    @pl.loop(1, parts)
    def _(i):
        greet(lax.rem(me + i, parts), shift)

    @pl.when(has_prev)
    def _():
        @pl.loop(0, parts)
        def _(i):
            greet(lax.rem(me + i, parts), prev)

    @pl.when(has_next)
    def _():
        @pl.loop(0, parts)
        def _(i):
            greet(lax.rem(me + i, parts), shift + 1)

    for i in range(1, shifts):
        greet(me, lax.rem(shift + i, shifts))

    level_of = [levels[b] for b in range(blocks)]
    places = []
    for b in range(blocks):
        place = level_of[b] * MAXB
        for a in range(b):
            place = place + jnp.where(level_of[a] == level_of[b], 1, 0)
        places.append(place)
        table[LEVELS * MAXB + b] = place

    @pl.loop(0, LEVELS * MAXB)
    def _(i):
        block = jnp.int32(0)
        for b in range(1, blocks):
            block = block + jnp.where(places[b] == i, b, 0)
        table[i] = block

    loads[0].wait()
    loads[1].wait()
    value = cot[...]
    high = value.astype(jnp.bfloat16)
    cot2[pl.ds(0, days), :] = high
    cot2[pl.ds(days, days), :] = (value - high.astype(jnp.float32)).astype(jnp.bfloat16)
    reach = gauge[...]
    gpos[...] = tile_of(reach)[0] * BLK + (reach & (BLK - 1))

    @pl.when(shift == shifts - 1)
    def _():
        xrecv[0] = jnp.zeros_like(xrecv[0])
        adj[pl.ds(days, HALO)] = jnp.zeros((HALO, TILES, LANES), jnp.float32)

    seeds(0)
    xsend[0] = seed[0]
    greeted = parts - 1 + shifts - 1
    greeted = greeted + parts * (has_prev.astype(jnp.int32) + has_next.astype(jnp.int32))
    pl.semaphore_wait(barrier, greeted)
    send_halo(0)
    for copy in loads[2:]:
        copy.wait()
    wanted = jnp.maximum(send[...], 0)
    wanted_tile = tile_of(wanted)[1]
    for h in range(LEVELS - 1):
        wlane[h] = jnp.broadcast_to(wanted[h : h + 1, :] & (LANES - 1), (8, LANES))
        wtile[h] = jnp.broadcast_to(wanted_tile[h : h + 1, :], (8, LANES))
    turn[...] = jnp.zeros_like(turn)
    pltpu.make_async_copy(staged, staged, load_sem.at[len(loads)]).wait()
    prepare(0)
    prepare(1)
    seeds(1)
    take_halo(0)
    adj[pl.ds(0, days)] = xsend[0]
    adj[pl.ds(days, HALO)] = xrecv[0]

    @pl.loop(0, LEVELS - 1)
    def _(h):
        routed(h)
        outgoing(h)
        send_slots(h)
        local_part(h + 1)
        send_halo(h + 1)
        gradient(h)
        send_grads(h)
        keep(h)

        @pl.when(h < LEVELS - 2)
        def _():
            seeds(h + 2)

        prepare(jnp.minimum(h + 2, LEVELS - 1))
        wait_bytes(own_msg.at[h, pl.ds(0, parts - 1)], ro.at[h])
        unpack(h, own_msg, rows_own)
        for t in range(days):
            adj[t] = xsend[h + 1, t] + remote_part(h + 1, rows_own[t : t + 1, :])

        @pl.when(has_next)
        def _():
            wait_bytes(far_msg.at[h, pl.ds(0, parts - 1)], rf.at[h])
            unpack(h, far_msg, rows_far)
            take_halo(h + 1)
            for t in range(HALO):
                adj[days + t] = xrecv[h + 1, t] + remote_part(h + 1, rows_far[t : t + 1, :])

    last = LEVELS - 1
    gradient(last)
    send_grads(last)
    routed(last)
    keep(last)
    for b in range(blocks):
        place = table[LEVELS * MAXB + b]
        for j in range(2):
            lat[:, pl.ds(b * BLK + j * LANES, LANES)] = lat_lv[place * 2 + j]

    @pl.loop(0, LEVELS)
    def _(h):
        wait_bytes(precv.at[h], rp.at[h])
        total = psend[h]
        for i in range(shifts - 1):
            total = total + precv[h, i]
        for r in range(2):
            ptotal[r, pl.ds(pl.multiple_of(h * TILES, TILES), TILES), :] = total[r]

    for b in range(blocks):
        place = table[LEVELS * MAXB + b]
        for j in range(2):
            for r in range(2):
                line = ptotal[r, pl.ds(place * 2 + j, 1), :]
                par[r : r + 1, pl.ds(b * BLK + j * LANES, LANES)] = line

    @pl.loop(0, LEVELS)
    def _(h):
        wait_bytes(precv.at[h], sp.at[h])

        @pl.when(has_prev)
        def _():
            wait_bytes(xsend.at[h, pl.ds(0, HALO)], sx.at[h])

    @pl.loop(0, LEVELS - 1)
    def _(h):
        wait_bytes(out_msg.at[h, pl.ds(0, parts - 1)], so.at[h])

        @pl.when(has_prev)
        def _():
            wait_bytes(out_msg.at[h, pl.ds(0, parts - 1)], sf.at[h])


def shards(parts, shifts, inflow, cotangent, gauge_reach, shape_param, scale_param, block_level, down_local, in_slot, send_reach):
    days, reaches = inflow.shape
    gauges = cotangent.shape[1]
    lines = reaches // LANES
    send = send_reach[0]
    if send.shape[1] < LANES:
        send = jnp.pad(send, ((0, 0), (0, LANES - send.shape[1])))
    f32, i32 = jnp.float32, jnp.int32
    levels = LEVELS
    rounds = LEVELS - 1
    tile = (TILES, LANES)
    vmem = pl.BlockSpec(memory_space=pltpu.VMEM)
    hbm = pl.BlockSpec(memory_space=pltpu.HBM)
    dma = pltpu.SemaphoreType.DMA
    return pl.pallas_call(
        functools.partial(adjoint_kernel, parts, shifts, days),
        out_shape=(
            jax.ShapeDtypeStruct((days, reaches), f32),
            jax.ShapeDtypeStruct((2, reaches), f32),
        ),
        in_specs=[pl.BlockSpec(memory_space=pltpu.SMEM)] + [hbm] * 8,
        out_specs=(vmem, vmem),
        scratch_shapes=[
            pltpu.SMEM((LEVELS * MAXB + block_level.shape[0],), i32),
            pltpu.VMEM((days, gauges), f32),
            pltpu.VMEM((1, gauges), i32),
            pltpu.VMEM((lines, LANES), f32),
            pltpu.VMEM((lines, LANES), f32),
            pltpu.VMEM((lines, LANES), i32),
            pltpu.VMEM((lines, LANES), i32),
            pltpu.VMEM(send.shape, i32),
            dma((8,)),
            pltpu.VMEM((2 * days, gauges), jnp.bfloat16),
            pltpu.VMEM((1, gauges), i32),
            pltpu.VMEM((levels, days) + tile, f32),
            pltpu.VMEM((days,) + tile, f32),
            pltpu.VMEM((levels, LAGS) + tile, f32),
            pltpu.VMEM((levels,) + tile, i32),
            pltpu.VMEM((levels,) + tile, i32),
            pltpu.VMEM((levels,) + tile, i32),
            pltpu.VMEM((rounds,) + tile, i32),
            pltpu.VMEM((rounds,) + tile, i32),
            pltpu.VMEM((levels,) + tile, f32),
            pltpu.VMEM((days + HALO,) + tile, f32),
            pltpu.VMEM((days,) + tile, f32),
            pltpu.VMEM((levels, days) + tile, f32),
            pltpu.VMEM((levels, HALO) + tile, f32),
            pltpu.VMEM((rounds, parts, 1, LANES), f32),
            pltpu.VMEM((rounds, parts, 1, LANES), f32),
            pltpu.VMEM((rounds, parts, 1, LANES), f32),
            pltpu.VMEM((2, LANES, LANES), f32),
            pltpu.VMEM((days, LANES), f32),
            pltpu.VMEM((days, LANES), f32),
            pltpu.VMEM((LAGS,) + tile, f32),
            pltpu.VMEM((levels, 2) + tile, f32),
            pltpu.VMEM((levels, shifts - 1, 2) + tile, f32),
            pltpu.VMEM((2, levels * TILES, LANES), f32),
            pltpu.VMEM((levels * TILES, days, LANES), f32),
            pltpu.VMEM((lines, days, LANES), f32),
            dma((levels,)),
            dma((levels,)),
            dma((rounds,)),
            dma((rounds,)),
            dma((rounds,)),
            dma((rounds,)),
            dma((levels,)),
            dma((levels,)),
        ],
        compiler_params=pltpu.CompilerParams(
            collective_id=0, has_side_effects=True, vmem_limit_bytes=40 * 1024 * 1024
        ),
    )(
        block_level,
        cotangent,
        gauge_reach.reshape(1, gauges),
        inflow,
        shape_param.reshape(lines, LANES),
        scale_param.reshape(lines, LANES),
        down_local.reshape(lines, LANES),
        in_slot.reshape(lines, LANES),
        send,
    )


def solution(mesh):
    in_specs = (
        P("tm", "basin"),
        P("tm", "basin"),
        P("basin"),
        P("basin"),
        P("basin"),
        P("basin"),
        P("basin"),
        P("basin"),
        P("basin", None, None),
    )
    out_specs = (P("tm", "basin"), P(None, "basin"))
    body = functools.partial(shards, mesh.shape["basin"], mesh.shape["tm"])
    return jax.shard_map(body, mesh=mesh, in_specs=in_specs, out_specs=out_specs, check_vma=False)
```

```python
import functools
import math

import jax
import jax.numpy as jnp
from jax import lax
from jax.experimental import pallas as pl
from jax.experimental.pallas import tpu as pltpu
from jax.sharding import PartitionSpec as P

BLK = 256
LAGS = 30
LEVELS = 8
MAXB = 4
CAP = 4
LANES = 128
TILES = MAXB * BLK // LANES
HALO = LAGS - 1
UNROLL = 32
OFFSETS = [k + 0.5 for k in range(LAGS)]
LOGS = [math.log(o) for o in OFFSETS]


def adjoint_kernel(
    parts,
    shifts,
    days,
    levels,
    cot_h,
    gauge_h,
    inflow_h,
    shape_h,
    scale_h,
    down_h,
    inslot_h,
    send_h,
    lat,
    par,
    table,
    cot,
    gauge,
    shape_p,
    scale_p,
    down,
    inslot,
    send,
    load_sem,
    cot2,
    gpos,
    seed,
    infl,
    kern,
    dlane,
    dtile,
    rlane,
    wlane,
    wtile,
    scl_lv,
    adj,
    lday,
    xsend,
    xrecv,
    out_msg,
    own_msg,
    far_msg,
    turn,
    rows_own,
    rows_far,
    lag_sum,
    psend,
    precv,
    plast,
    gsum,
    gall,
    ptotal,
    lat_lv,
    staged,
    sx,
    rx,
    so,
    sf,
    ro,
    rf,
    sp,
    rp,
):
    blocks = levels.shape[0]
    me = lax.axis_index("basin")
    shift = lax.axis_index("tm")
    prev = lax.rem(shift + shifts - 1, shifts)
    has_next = shift < shifts - 1
    has_prev = shift > 0
    side = max(1, math.isqrt(parts // 2))
    hops = [min(d, side - d) for d in range(side)]
    routes = [(y, x, c) for y in range(side) for x in range(side) for c in range(2)][1:]
    routes.sort(key=lambda r: -(hops[r[0]] + hops[r[1]]))

    def partner(route):
        y = lax.rem(me // (2 * side) + route[0], side)
        x = lax.rem(lax.rem(me // 2, side) + route[1], side)
        return (y * side + x) * 2 + lax.rem(me + route[2], 2)


    def tile_of(reach):
        block = reach >> 8
        slot = jnp.zeros_like(reach)
        for b in range(blocks):
            slot = jnp.where(block == b, table[LEVELS * MAXB + b], slot)
        return slot, (slot & (MAXB - 1)) * 2 + ((reach >> 7) & 1)

    def prepare(h):
        spots = [table[h * MAXB + m] * 2 + j for m in range(MAXB) for j in range(2)]

        def tiled(ref):
            return jnp.concatenate([ref[pl.ds(i, 1), :] for i in spots], axis=0)

        target = tiled(down)
        dtile[h] = jnp.where(target >= 0, tile_of(target)[1], -1)
        dlane[h] = target & (LANES - 1)
        rlane[h] = tiled(inslot)
        shp = tiled(shape_p) - 1.0
        scl = tiled(scale_p)
        scl_lv[h] = scl
        weights = [jnp.exp(shp * LOGS[k] - OFFSETS[k] / scl) for k in range(LAGS)]
        total = weights[0]
        for k in range(1, LAGS):
            total = total + weights[k]
        for k in range(LAGS):
            kern[h, k] = weights[k] / total

    def seeds(h):
        width = 2 * LANES
        local = gpos[...] - h * (MAXB * BLK)

        ids = lax.broadcasted_iota(jnp.int32, (width, local.shape[1]), 0)
        for c in range(MAXB * BLK // width):
            hot = jnp.where(ids == local - c * width, 1.0, 0.0).astype(jnp.bfloat16)
            both = lax.dot_general(
                cot2[...], hot, (((1,), (1,)), ((), ())), preferred_element_type=jnp.float32
            )
            sums = both[:days] + both[days:]
            for j in range(width // LANES):
                seed[h, :, 2 * c + j, :] = sums[:, j * LANES : (j + 1) * LANES]

    def routed(h):
        total = kern[h, 0][None] * adj[pl.ds(0, days)]
        for k in range(1, LAGS):
            total = total + kern[h, k][None] * adj[pl.ds(k, days)]
        lday[...] = total

    def outgoing(h):
        lane, tile = wlane[h], wtile[h]
        for g in range(days // 8):
            picked = jnp.zeros((8, LANES), jnp.float32)
            for s in range(TILES):
                got = jnp.take_along_axis(lday[pl.ds(8 * g, 8), s, :], lane, axis=1)
                picked = jnp.where(tile == s, got, picked)
            turn[0, 8 * g : 8 * g + 8, :] = picked
        turn[0] = jnp.transpose(turn[0])
        lanes = lax.broadcasted_iota(jnp.int32, (parts, LANES), 1)
        packed = jnp.zeros((parts, LANES), jnp.float32)
        for c in range(CAP):
            piece = turn[0, pl.ds(c, parts, stride=CAP), :]
            piece = pltpu.roll(piece, c * days, axis=1) if c else piece
            packed = jnp.where((lanes >= c * days) & (lanes < (c + 1) * days), piece, packed)
        out_msg[h, :, 0, :] = packed

    def slot_copy(h, q, target, ssem, buf, rsem):
        return pltpu.make_async_remote_copy(
            src_ref=out_msg.at[h, q],
            dst_ref=buf.at[h, me],
            send_sem=ssem.at[h],
            recv_sem=rsem.at[h],
            device_id={"basin": q, "tm": target},
            device_id_type=pl.DeviceIdType.MESH,
        )

    def send_slots(h):
        @pl.when(has_prev)
        def _():
            for i in routes:
                slot_copy(h, partner(i), prev, sf, far_msg, rf).start()
                slot_copy(h, partner(i), shift, so, own_msg, ro).start()

        @pl.when(jnp.logical_not(has_prev))
        def _():
            for i in routes:
                slot_copy(h, partner(i), shift, so, own_msg, ro).start()

    def local_part(h):
        lane, tile = dlane[h], dtile[h]
        masks = [tile == s for s in range(TILES)]

        @pl.loop(0, days, unroll=UNROLL)
        def _(t):
            got = jnp.zeros((TILES, LANES), jnp.float32)
            for s in range(TILES):
                line = jnp.broadcast_to(lday[t, s : s + 1, :], (TILES, LANES))
                got = jnp.where(masks[s], jnp.take_along_axis(line, lane, axis=1), got)
            xsend[h, t] = seed[h, t] + got

    def halo_copy(h):
        return pltpu.make_async_remote_copy(
            src_ref=xsend.at[h, pl.ds(0, HALO)],
            dst_ref=xrecv.at[h],
            send_sem=sx.at[h],
            recv_sem=rx.at[h],
            device_id={"basin": me, "tm": prev},
            device_id_type=pl.DeviceIdType.MESH,
        )

    def send_halo(h):
        @pl.when(has_prev)
        def _():
            halo_copy(h).start()

    def take_halo(h):
        @pl.when(has_next)
        def _():
            halo_copy(h).wait_recv()

    def unpack(h, buf, rows):
        arrived = buf[h, :, 0, :]
        for c in range(CAP):
            piece = pltpu.roll(arrived, LANES - c * days, axis=1) if c else arrived
            turn[1, pl.ds(c, parts, stride=CAP), :] = piece
        rows[...] = jnp.transpose(turn[1])[: rows.shape[0]]

    def remote_part(h, row):
        slot = rlane[h]
        line = jnp.broadcast_to(row, (TILES, LANES))
        got = jnp.take_along_axis(line, slot & (LANES - 1), axis=1)
        return jnp.where(slot >= 0, got, 0.0)

    def gradient(h):
        for m in range(MAXB):
            block = table[h * MAXB + m]
            for j in range(2):
                infl[:, 2 * m + j, :] = staged[block * 2 + j]
        for k in range(LAGS):
            lag_sum[k] = jnp.sum(infl[...] * adj[pl.ds(k, days)], axis=0)
        mean = kern[h, 0] * lag_sum[0]
        for k in range(1, LAGS):
            mean = mean + kern[h, k] * lag_sum[k]
        first = jnp.zeros((TILES, LANES), jnp.float32)
        second = jnp.zeros((TILES, LANES), jnp.float32)
        for k in range(LAGS):
            logit = kern[h, k] * (lag_sum[k] - mean)
            first = first + logit * LOGS[k]
            second = second + logit * OFFSETS[k]
        scl = scl_lv[h]
        psend[h, :, 0, 0, :] = first
        psend[h, :, 1, 0, :] = second / (scl * scl)

    def peer_copy(src, dst, h, i):
        return pltpu.make_async_remote_copy(
            src_ref=src,
            dst_ref=dst,
            send_sem=sp.at[h],
            recv_sem=rp.at[h],
            device_id={"basin": me, "tm": lax.rem(shift + i, shifts)},
            device_id_type=pl.DeviceIdType.MESH,
        )

    def send_grads(h):
        for i in range(1, shifts):
            owner = lax.rem(shift + i, shifts)
            peer_copy(psend.at[h, owner], precv.at[h, i - 1], h, i).start()

    def keep(h):
        for s in range(TILES):
            lat_lv[h * TILES + s] = lday[:, s, :]

    def wait_bytes(ref, sem):
        pltpu.make_async_copy(ref, ref, sem).wait()

    barrier = pltpu.get_barrier_semaphore()

    def greet(q, k):
        where = {"basin": q, "tm": k}
        pl.semaphore_signal(barrier, inc=1, device_id=where, device_id_type=pl.DeviceIdType.MESH)

    loads = [
        pltpu.make_async_copy(src, dst, load_sem.at[i])
        for i, (src, dst) in enumerate(
            [(cot_h, cot), (gauge_h, gauge), (shape_h, shape_p), (scale_h, scale_p), (down_h, down), (inslot_h, inslot), (send_h, send)]
        )
    ]
    for copy in loads:
        copy.start()
    for i in range(2 * blocks):
        pltpu.make_async_copy(
            inflow_h.at[:, pl.ds(i * LANES, LANES)], staged.at[i], load_sem.at[len(loads)]
        ).start()

    @pl.loop(1, parts)
    def _(i):
        greet(lax.rem(me + i, parts), shift)

    @pl.when(has_prev)
    def _():
        @pl.loop(0, parts)
        def _(i):
            greet(lax.rem(me + i, parts), prev)

    @pl.when(has_next)
    def _():
        @pl.loop(0, parts)
        def _(i):
            greet(lax.rem(me + i, parts), shift + 1)

    for i in range(1, shifts):
        greet(me, lax.rem(shift + i, shifts))

    level_of = [levels[b] for b in range(blocks)]
    places = []
    for b in range(blocks):
        place = level_of[b] * MAXB
        for a in range(b):
            place = place + jnp.where(level_of[a] == level_of[b], 1, 0)
        places.append(place)
        table[LEVELS * MAXB + b] = place

    @pl.loop(0, LEVELS * MAXB)
    def _(i):
        block = jnp.int32(0)
        for b in range(1, blocks):
            block = block + jnp.where(places[b] == i, b, 0)
        table[i] = block

    loads[0].wait()
    loads[1].wait()
    value = cot[...]
    high = value.astype(jnp.bfloat16)
    cot2[pl.ds(0, days), :] = high
    cot2[pl.ds(days, days), :] = (value - high.astype(jnp.float32)).astype(jnp.bfloat16)
    reach = gauge[...]
    gpos[...] = tile_of(reach)[0] * BLK + (reach & (BLK - 1))

    @pl.when(shift == shifts - 1)
    def _():
        xrecv[0] = jnp.zeros_like(xrecv[0])
        adj[pl.ds(days, HALO)] = jnp.zeros((HALO, TILES, LANES), jnp.float32)

    seeds(0)
    xsend[0] = seed[0]
    greeted = parts - 1 + shifts - 1
    greeted = greeted + parts * (has_prev.astype(jnp.int32) + has_next.astype(jnp.int32))
    pl.semaphore_wait(barrier, greeted)
    send_halo(0)
    for copy in loads[2:]:
        copy.wait()
    for h in range(LEVELS - 1):
        wanted = jnp.broadcast_to(jnp.maximum(send[h], 0), (8, LANES))
        wlane[h] = wanted & (LANES - 1)
        wtile[h] = tile_of(wanted)[1]
    turn[...] = jnp.zeros_like(turn)
    pltpu.make_async_copy(staged, staged, load_sem.at[len(loads)]).wait()
    prepare(0)
    prepare(1)
    seeds(1)
    take_halo(0)
    adj[pl.ds(0, days)] = xsend[0]
    adj[pl.ds(days, HALO)] = xrecv[0]

    @pl.loop(0, LEVELS - 1)
    def _(h):
        routed(h)
        outgoing(h)
        send_slots(h)
        local_part(h + 1)
        send_halo(h + 1)
        gradient(h)
        send_grads(h)
        keep(h)

        @pl.when(h < LEVELS - 2)
        def _():
            seeds(h + 2)

        prepare(jnp.minimum(h + 2, LEVELS - 1))
        wait_bytes(own_msg.at[h, pl.ds(0, parts - 1)], ro.at[h])
        unpack(h, own_msg, rows_own)
        for t in range(days):
            adj[t] = xsend[h + 1, t] + remote_part(h + 1, rows_own[t : t + 1, :])

        @pl.when(has_next)
        def _():
            wait_bytes(far_msg.at[h, pl.ds(0, parts - 1)], rf.at[h])
            unpack(h, far_msg, rows_far)
            take_halo(h + 1)
            for t in range(HALO):
                adj[days + t] = xrecv[h + 1, t] + remote_part(h + 1, rows_far[t : t + 1, :])

    last = LEVELS - 1
    gradient(last)
    for i in range(1, shifts):
        peer_copy(psend.at[last], plast.at[i - 1], last, i).start()

    @pl.loop(0, last)
    def _(h):
        wait_bytes(precv.at[h], rp.at[h])
        total = psend[h, shift]
        for i in range(shifts - 1):
            total = total + precv[h, i]
        gsum[h] = total

    for i in range(1, shifts):
        peer_copy(gsum, gall.at[shift], LEVELS, i).start()
    gall[shift] = gsum[...]
    routed(last)
    keep(last)
    for b in range(blocks):
        place = table[LEVELS * MAXB + b]
        for j in range(2):
            lat[:, pl.ds(b * BLK + j * LANES, LANES)] = lat_lv[place * 2 + j]
    wait_bytes(gall.at[pl.ds(0, shifts - 1)], rp.at[LEVELS])
    for h in range(last):
        for r in range(2):
            ptotal[r, h * TILES : (h + 1) * TILES, :] = gall[:, h, r, 0, :]
    wait_bytes(plast, rp.at[last])
    for r in range(2):
        total = psend[last, :, r, 0, :]
        for i in range(shifts - 1):
            total = total + plast[i, :, r, 0, :]
        ptotal[r, last * TILES : LEVELS * TILES, :] = total

    for b in range(blocks):
        place = table[LEVELS * MAXB + b]
        for j in range(2):
            for r in range(2):
                line = ptotal[r, pl.ds(place * 2 + j, 1), :]
                par[r : r + 1, pl.ds(b * BLK + j * LANES, LANES)] = line

    @pl.loop(0, LEVELS)
    def _(h):

        @pl.when(has_prev)
        def _():
            wait_bytes(xsend.at[h, pl.ds(0, HALO)], sx.at[h])

    @pl.loop(0, LEVELS - 1)
    def _(h):
        wait_bytes(out_msg.at[h, pl.ds(0, parts - 1)], so.at[h])
        wait_bytes(precv.at[h], sp.at[h])

        @pl.when(has_prev)
        def _():
            wait_bytes(out_msg.at[h, pl.ds(0, parts - 1)], sf.at[h])
    wait_bytes(plast, sp.at[last])
    wait_bytes(gall.at[pl.ds(0, shifts - 1)], sp.at[LEVELS])


def shards(parts, shifts, inflow, cotangent, gauge_reach, shape_param, scale_param, block_level, down_local, in_slot, send_reach):
    days, reaches = inflow.shape
    gauges = cotangent.shape[1]
    lines = reaches // LANES
    send = send_reach
    if send.shape[2] < LANES:
        send = jnp.pad(send, ((0, 0), (0, 0), (0, LANES - send.shape[2])))
    f32, i32 = jnp.float32, jnp.int32
    levels = LEVELS
    rounds = LEVELS - 1
    tile = (TILES, LANES)
    vmem = pl.BlockSpec(memory_space=pltpu.VMEM)
    hbm = pl.BlockSpec(memory_space=pltpu.HBM)
    dma = pltpu.SemaphoreType.DMA
    return pl.pallas_call(
        functools.partial(adjoint_kernel, parts, shifts, days),
        out_shape=(
            jax.ShapeDtypeStruct((days, reaches), f32),
            jax.ShapeDtypeStruct((2, reaches), f32),
        ),
        in_specs=[pl.BlockSpec(memory_space=pltpu.SMEM)] + [hbm] * 8,
        out_specs=(vmem, vmem),
        scratch_shapes=[
            pltpu.SMEM((LEVELS * MAXB + block_level.shape[0],), i32),
            pltpu.VMEM((days, gauges), f32),
            pltpu.VMEM((1, gauges), i32),
            pltpu.VMEM((lines, LANES), f32),
            pltpu.VMEM((lines, LANES), f32),
            pltpu.VMEM((lines, LANES), i32),
            pltpu.VMEM((lines, LANES), i32),
            pltpu.VMEM((send.shape[1], 1, LANES), i32),
            dma((8,)),
            pltpu.VMEM((2 * days, gauges), jnp.bfloat16),
            pltpu.VMEM((1, gauges), i32),
            pltpu.VMEM((levels, days) + tile, f32),
            pltpu.VMEM((days,) + tile, f32),
            pltpu.VMEM((levels, LAGS) + tile, f32),
            pltpu.VMEM((levels,) + tile, i32),
            pltpu.VMEM((levels,) + tile, i32),
            pltpu.VMEM((levels,) + tile, i32),
            pltpu.VMEM((rounds,) + tile, i32),
            pltpu.VMEM((rounds,) + tile, i32),
            pltpu.VMEM((levels,) + tile, f32),
            pltpu.VMEM((days + HALO,) + tile, f32),
            pltpu.VMEM((days,) + tile, f32),
            pltpu.VMEM((levels, days) + tile, f32),
            pltpu.VMEM((levels, HALO) + tile, f32),
            pltpu.VMEM((rounds, parts, 1, LANES), f32),
            pltpu.VMEM((rounds, parts, 1, LANES), f32),
            pltpu.VMEM((rounds, parts, 1, LANES), f32),
            pltpu.VMEM((2, LANES, LANES), f32),
            pltpu.VMEM((days, LANES), f32),
            pltpu.VMEM((days, LANES), f32),
            pltpu.VMEM((LAGS,) + tile, f32),
            pltpu.VMEM((levels, TILES, 2, 1, LANES), f32),
            pltpu.VMEM((rounds, shifts - 1, 2, 1, LANES), f32),
            pltpu.VMEM((shifts - 1, TILES, 2, 1, LANES), f32),
            pltpu.VMEM((rounds, 2, 1, LANES), f32),
            pltpu.VMEM((shifts, rounds, 2, 1, LANES), f32),
            pltpu.VMEM((2, levels * TILES, LANES), f32),
            pltpu.VMEM((levels * TILES, days, LANES), f32),
            pltpu.VMEM((lines, days, LANES), f32),
            dma((levels,)),
            dma((levels,)),
            dma((rounds,)),
            dma((rounds,)),
            dma((rounds,)),
            dma((rounds,)),
            dma((levels + 1,)),
            dma((levels + 1,)),
        ],
        compiler_params=pltpu.CompilerParams(
            collective_id=0, has_side_effects=True, vmem_limit_bytes=66000000
        ),
    )(
        block_level,
        cotangent,
        gauge_reach.reshape(1, gauges),
        inflow,
        shape_param.reshape(lines, LANES),
        scale_param.reshape(lines, LANES),
        down_local.reshape(lines, LANES),
        in_slot.reshape(lines, LANES),
        jnp.transpose(send, (1, 0, 2)),
    )


def solution(mesh):
    in_specs = (
        P("tm", "basin"),
        P("tm", "basin"),
        P("basin"),
        P("basin"),
        P("basin"),
        P("basin"),
        P("basin"),
        P("basin"),
        P("basin", None, None),
    )
    out_specs = (P("tm", "basin"), P(None, "basin"))
    body = functools.partial(shards, mesh.shape["basin"], mesh.shape["tm"])
    return jax.shard_map(body, mesh=mesh, in_specs=in_specs, out_specs=out_specs, check_vma=False)
```

```python
import functools
import math

import jax
import jax.numpy as jnp
from jax import lax
from jax.experimental import pallas as pl
from jax.experimental.pallas import tpu as pltpu
from jax.sharding import PartitionSpec as P

BLK = 256
LAGS = 30
LEVELS = 8
MAXB = 4
CAP = 4
LANES = 128
TILES = MAXB * BLK // LANES
HALO = LAGS - 1
OFFSETS = [k + 0.5 for k in range(LAGS)]
LOGS = [math.log(o) for o in OFFSETS]


def adjoint_kernel(
    parts,
    shifts,
    days,
    levels,
    cot_h,
    gauge_h,
    inflow_h,
    shape_h,
    scale_h,
    down_h,
    inslot_h,
    send_h,
    lat,
    par,
    table,
    cot,
    gauge,
    shape_p,
    scale_p,
    down,
    inslot,
    send,
    load_sem,
    cot2,
    gpos,
    seed,
    infl,
    kern,
    dlane,
    dtile,
    rlane,
    wlane,
    wtile,
    scl_lv,
    adj,
    lday,
    xsend,
    xrecv,
    out_msg,
    own_msg,
    far_msg,
    turn,
    rows_own,
    rows_far,
    lag_sum,
    psend,
    precv,
    plast,
    gsum,
    gall,
    ptotal,
    lat_lv,
    staged,
    sx,
    rx,
    so,
    sf,
    ro,
    rf,
    sp,
    rp,
):
    blocks = levels.shape[0]
    me = lax.axis_index("basin")
    shift = lax.axis_index("tm")
    prev = lax.rem(shift + shifts - 1, shifts)
    has_next = shift < shifts - 1
    has_prev = shift > 0
    side = max(1, math.isqrt(parts // 2))
    hops = [min(d, side - d) for d in range(side)]
    routes = [(y, x, c) for y in range(side) for x in range(side) for c in range(2)][1:]
    routes.sort(key=lambda r: -(hops[r[0]] + hops[r[1]]))

    def partner(route):
        y = lax.rem(me // (2 * side) + route[0], side)
        x = lax.rem(lax.rem(me // 2, side) + route[1], side)
        return (y * side + x) * 2 + lax.rem(me + route[2], 2)


    def tile_of(reach):
        block = reach >> 8
        slot = jnp.zeros_like(reach)
        for b in range(blocks):
            slot = jnp.where(block == b, table[LEVELS * MAXB + b], slot)
        return slot, (slot & (MAXB - 1)) * 2 + ((reach >> 7) & 1)

    def prepare(h):
        spots = [table[h * MAXB + m] * 2 + j for m in range(MAXB) for j in range(2)]

        def tiled(ref):
            return jnp.concatenate([ref[pl.ds(i, 1), :] for i in spots], axis=0)

        target = tiled(down)
        dtile[h] = jnp.where(target >= 0, tile_of(target)[1], -1)
        dlane[h] = target & (LANES - 1)
        rlane[h] = tiled(inslot)
        shp = tiled(shape_p) - 1.0
        scl = tiled(scale_p)
        scl_lv[h] = scl
        weights = [jnp.exp(shp * LOGS[k] - OFFSETS[k] / scl) for k in range(LAGS)]
        total = weights[0]
        for k in range(1, LAGS):
            total = total + weights[k]
        for k in range(LAGS):
            kern[h, k] = weights[k] / total

    def seeds(h):
        width = 2 * LANES
        local = gpos[...] - h * (MAXB * BLK)

        ids = lax.broadcasted_iota(jnp.int32, (width, local.shape[1]), 0)
        for c in range(MAXB * BLK // width):
            hot = jnp.where(ids == local - c * width, 1.0, 0.0).astype(jnp.bfloat16)
            both = lax.dot_general(
                cot2[...], hot, (((1,), (1,)), ((), ())), preferred_element_type=jnp.float32
            )
            sums = both[:days] + both[days:]
            for j in range(width // LANES):
                seed[h, :, 2 * c + j, :] = sums[:, j * LANES : (j + 1) * LANES]

    def routed_own(h):
        for g in range(0, days, 8):
            total = kern[h, 0][None] * adj[pl.ds(g, 8)]
            for k in range(1, min(LAGS, days - 7 - g)):
                total = total + kern[h, k][None] * adj[pl.ds(g + k, 8)]
            lday[pl.ds(g, 8)] = total

    def routed_far(h):
        for g in range(0, days, 8):
            total = lday[pl.ds(g, 8)]
            for k in range(days - 7 - g, LAGS):
                total = total + kern[h, k][None] * adj[pl.ds(g + k, 8)]
            lday[pl.ds(g, 8)] = total

    def outgoing(h):
        lane, tile = wlane[h], wtile[h]
        for g in range(days // 8):
            picked = jnp.zeros((8, LANES), jnp.float32)
            for s in range(TILES):
                got = jnp.take_along_axis(lday[pl.ds(8 * g, 8), s, :], lane, axis=1)
                picked = jnp.where(tile == s, got, picked)
            turn[0, 8 * g : 8 * g + 8, :] = picked
        turn[0] = jnp.transpose(turn[0])
        lanes = lax.broadcasted_iota(jnp.int32, (parts, LANES), 1)
        packed = jnp.zeros((parts, LANES), jnp.float32)
        for c in range(CAP):
            piece = turn[0, pl.ds(c, parts, stride=CAP), :]
            piece = pltpu.roll(piece, c * days, axis=1) if c else piece
            packed = jnp.where((lanes >= c * days) & (lanes < (c + 1) * days), piece, packed)
        out_msg[h, :, 0, :] = packed

    def slot_copy(h, q, target, ssem, buf, rsem):
        return pltpu.make_async_remote_copy(
            src_ref=out_msg.at[h, q],
            dst_ref=buf.at[h, me],
            send_sem=ssem.at[h],
            recv_sem=rsem.at[h],
            device_id={"basin": q, "tm": target},
            device_id_type=pl.DeviceIdType.MESH,
        )

    def send_slots(h):
        @pl.when(has_prev)
        def _():
            for i in routes:
                slot_copy(h, partner(i), prev, sf, far_msg, rf).start()
                slot_copy(h, partner(i), shift, so, own_msg, ro).start()

        @pl.when(jnp.logical_not(has_prev))
        def _():
            for i in routes:
                slot_copy(h, partner(i), shift, so, own_msg, ro).start()

    def local_part(h, first, count):
        lane, tile = dlane[h], dtile[h]
        masks = [tile == s for s in range(TILES)]
        for t in range(first, first + count):
            got = jnp.zeros((TILES, LANES), jnp.float32)
            for s in range(TILES):
                line = jnp.broadcast_to(lday[t, s : s + 1, :], (TILES, LANES))
                got = jnp.where(masks[s], jnp.take_along_axis(line, lane, axis=1), got)
            xsend[h, t] = seed[h, t] + got

    def halo_copy(h, first, count):
        return pltpu.make_async_remote_copy(
            src_ref=xsend.at[h, pl.ds(first, count)],
            dst_ref=xrecv.at[h, pl.ds(first, count)],
            send_sem=sx.at[h],
            recv_sem=rx.at[h],
            device_id={"basin": me, "tm": prev},
            device_id_type=pl.DeviceIdType.MESH,
        )

    def send_halo(h, first, count):
        @pl.when(has_prev)
        def _():
            halo_copy(h, first, count).start()

    def take_halo(h):
        @pl.when(has_next)
        def _():
            wait_bytes(xrecv.at[h], rx.at[h])

    def unpack(h, buf, rows):
        arrived = buf[h, :, 0, :]
        for c in range(CAP):
            piece = pltpu.roll(arrived, LANES - c * days, axis=1) if c else arrived
            turn[1, pl.ds(c, parts, stride=CAP), :] = piece
        rows[...] = jnp.transpose(turn[1])[: rows.shape[0]]

    def remote_part(h, row):
        slot = rlane[h]
        line = jnp.broadcast_to(row, (TILES, LANES))
        got = jnp.take_along_axis(line, slot & (LANES - 1), axis=1)
        return jnp.where(slot >= 0, got, 0.0)

    def gradient(h):
        for m in range(MAXB):
            block = table[h * MAXB + m]
            for j in range(2):
                infl[:, 2 * m + j, :] = staged[block * 2 + j]
        for k in range(LAGS):
            lag_sum[k] = jnp.sum(infl[...] * adj[pl.ds(k, days)], axis=0)
        mean = kern[h, 0] * lag_sum[0]
        for k in range(1, LAGS):
            mean = mean + kern[h, k] * lag_sum[k]
        first = jnp.zeros((TILES, LANES), jnp.float32)
        second = jnp.zeros((TILES, LANES), jnp.float32)
        for k in range(LAGS):
            logit = kern[h, k] * (lag_sum[k] - mean)
            first = first + logit * LOGS[k]
            second = second + logit * OFFSETS[k]
        scl = scl_lv[h]
        psend[h, :, 0, 0, :] = first
        psend[h, :, 1, 0, :] = second / (scl * scl)

    def peer_copy(src, dst, h, i):
        return pltpu.make_async_remote_copy(
            src_ref=src,
            dst_ref=dst,
            send_sem=sp.at[h],
            recv_sem=rp.at[h],
            device_id={"basin": me, "tm": lax.rem(shift + i, shifts)},
            device_id_type=pl.DeviceIdType.MESH,
        )

    def send_grads(h):
        for i in range(1, shifts):
            owner = lax.rem(shift + i, shifts)
            peer_copy(psend.at[h, owner], precv.at[h, i - 1], h, i).start()

    def keep(h):
        for s in range(TILES):
            lat_lv[h * TILES + s] = lday[:, s, :]

    def wait_bytes(ref, sem):
        pltpu.make_async_copy(ref, ref, sem).wait()

    barrier = pltpu.get_barrier_semaphore()

    def greet(q, k):
        where = {"basin": q, "tm": k}
        pl.semaphore_signal(barrier, inc=1, device_id=where, device_id_type=pl.DeviceIdType.MESH)

    loads = [
        pltpu.make_async_copy(src, dst, load_sem.at[i])
        for i, (src, dst) in enumerate(
            [(cot_h, cot), (gauge_h, gauge), (shape_h, shape_p), (scale_h, scale_p), (down_h, down), (inslot_h, inslot), (send_h, send)]
        )
    ]
    for copy in loads:
        copy.start()
    for i in range(2 * blocks):
        pltpu.make_async_copy(
            inflow_h.at[:, pl.ds(i * LANES, LANES)], staged.at[i], load_sem.at[len(loads)]
        ).start()

    everyone = routes + [(0, 0, 0)]

    @pl.when(has_prev)
    def _():
        for i in everyone:
            greet(partner(i), prev)

    @pl.when(has_next)
    def _():
        for i in everyone:
            greet(partner(i), shift + 1)

    for i in routes:
        greet(partner(i), shift)
    for i in range(1, shifts):
        greet(me, lax.rem(shift + i, shifts))

    level_of = [levels[b] for b in range(blocks)]
    places = []
    for b in range(blocks):
        place = level_of[b] * MAXB
        for a in range(b):
            place = place + jnp.where(level_of[a] == level_of[b], 1, 0)
        places.append(place)
        table[LEVELS * MAXB + b] = place

    loads[0].wait()
    loads[1].wait()
    value = cot[...]
    high = value.astype(jnp.bfloat16)
    cot2[pl.ds(0, days), :] = high
    cot2[pl.ds(days, days), :] = (value - high.astype(jnp.float32)).astype(jnp.bfloat16)
    reach = gauge[...]
    gpos[...] = tile_of(reach)[0] * BLK + (reach & (BLK - 1))

    @pl.when(shift == shifts - 1)
    def _():
        xrecv[0] = jnp.zeros_like(xrecv[0])
        adj[pl.ds(days, HALO)] = jnp.zeros((HALO, TILES, LANES), jnp.float32)

    seeds(0)
    xsend[0] = seed[0]
    greeted = parts - 1 + shifts - 1
    greeted = greeted + parts * (has_prev.astype(jnp.int32) + has_next.astype(jnp.int32))
    pl.semaphore_wait(barrier, greeted)
    send_halo(0, 0, HALO)

    @pl.loop(0, LEVELS * MAXB)
    def _(i):
        block = jnp.int32(0)
        for b in range(1, blocks):
            block = block + jnp.where(places[b] == i, b, 0)
        table[i] = block

    for copy in loads[2:]:
        copy.wait()
    for h in range(LEVELS - 1):
        wanted = jnp.broadcast_to(jnp.maximum(send[h], 0), (8, LANES))
        wlane[h] = wanted & (LANES - 1)
        wtile[h] = tile_of(wanted)[1]
    turn[...] = jnp.zeros_like(turn)
    pltpu.make_async_copy(staged, staged, load_sem.at[len(loads)]).wait()
    prepare(0)
    prepare(1)
    seeds(1)
    adj[pl.ds(0, days)] = xsend[0]
    routed_own(0)
    take_halo(0)
    adj[pl.ds(days, HALO)] = xrecv[0]

    @pl.loop(0, LEVELS - 1)
    def _(h):
        routed_far(h)
        outgoing(h)
        send_slots(h)
        half = days // 2
        local_part(h + 1, 0, half)
        send_halo(h + 1, 0, half)
        local_part(h + 1, half, days - half)
        send_halo(h + 1, half, HALO - half)
        gradient(h)
        send_grads(h)
        keep(h)

        @pl.when(h < LEVELS - 2)
        def _():
            seeds(h + 2)

        prepare(jnp.minimum(h + 2, LEVELS - 1))
        wait_bytes(own_msg.at[h, pl.ds(0, parts - 1)], ro.at[h])
        unpack(h, own_msg, rows_own)
        for t in range(days):
            adj[t] = xsend[h + 1, t] + remote_part(h + 1, rows_own[t : t + 1, :])
        routed_own(h + 1)

        @pl.when(has_next)
        def _():
            wait_bytes(far_msg.at[h, pl.ds(0, parts - 1)], rf.at[h])
            unpack(h, far_msg, rows_far)
            take_halo(h + 1)
            for t in range(HALO):
                adj[days + t] = xrecv[h + 1, t] + remote_part(h + 1, rows_far[t : t + 1, :])

    last = LEVELS - 1
    gradient(last)
    for i in range(1, shifts):
        peer_copy(psend.at[last], plast.at[i - 1], last, i).start()

    @pl.loop(0, last)
    def _(h):
        wait_bytes(precv.at[h], rp.at[h])
        total = psend[h, shift]
        for i in range(shifts - 1):
            total = total + precv[h, i]
        gsum[h] = total

    for i in range(1, shifts):
        peer_copy(gsum, gall.at[shift], LEVELS, i).start()
    gall[shift] = gsum[...]
    routed_far(last)
    keep(last)
    for b in range(blocks):
        place = table[LEVELS * MAXB + b]
        for j in range(2):
            lat[:, pl.ds(b * BLK + j * LANES, LANES)] = lat_lv[place * 2 + j]
    wait_bytes(gall.at[pl.ds(0, shifts - 1)], rp.at[LEVELS])
    for h in range(last):
        for r in range(2):
            ptotal[r, h * TILES : (h + 1) * TILES, :] = gall[:, h, r, 0, :]
    wait_bytes(plast, rp.at[last])
    for r in range(2):
        total = psend[last, :, r, 0, :]
        for i in range(shifts - 1):
            total = total + plast[i, :, r, 0, :]
        ptotal[r, last * TILES : LEVELS * TILES, :] = total

    for b in range(blocks):
        place = table[LEVELS * MAXB + b]
        for j in range(2):
            for r in range(2):
                line = ptotal[r, pl.ds(place * 2 + j, 1), :]
                par[r : r + 1, pl.ds(b * BLK + j * LANES, LANES)] = line

    @pl.loop(0, LEVELS)
    def _(h):

        @pl.when(has_prev)
        def _():
            wait_bytes(xsend.at[h, pl.ds(0, HALO)], sx.at[h])

    @pl.loop(0, LEVELS - 1)
    def _(h):
        wait_bytes(out_msg.at[h, pl.ds(0, parts - 1)], so.at[h])
        wait_bytes(precv.at[h], sp.at[h])

        @pl.when(has_prev)
        def _():
            wait_bytes(out_msg.at[h, pl.ds(0, parts - 1)], sf.at[h])
    wait_bytes(plast, sp.at[last])
    wait_bytes(gall.at[pl.ds(0, shifts - 1)], sp.at[LEVELS])


def shards(parts, shifts, inflow, cotangent, gauge_reach, shape_param, scale_param, block_level, down_local, in_slot, send_reach):
    days, reaches = inflow.shape
    gauges = cotangent.shape[1]
    lines = reaches // LANES
    send = send_reach
    if send.shape[2] < LANES:
        send = jnp.pad(send, ((0, 0), (0, 0), (0, LANES - send.shape[2])))
    f32, i32 = jnp.float32, jnp.int32
    levels = LEVELS
    rounds = LEVELS - 1
    tile = (TILES, LANES)
    vmem = pl.BlockSpec(memory_space=pltpu.VMEM)
    hbm = pl.BlockSpec(memory_space=pltpu.HBM)
    dma = pltpu.SemaphoreType.DMA
    return pl.pallas_call(
        functools.partial(adjoint_kernel, parts, shifts, days),
        out_shape=(
            jax.ShapeDtypeStruct((days, reaches), f32),
            jax.ShapeDtypeStruct((2, reaches), f32),
        ),
        in_specs=[pl.BlockSpec(memory_space=pltpu.SMEM)] + [hbm] * 8,
        out_specs=(vmem, vmem),
        scratch_shapes=[
            pltpu.SMEM((LEVELS * MAXB + block_level.shape[0],), i32),
            pltpu.VMEM((days, gauges), f32),
            pltpu.VMEM((1, gauges), i32),
            pltpu.VMEM((lines, LANES), f32),
            pltpu.VMEM((lines, LANES), f32),
            pltpu.VMEM((lines, LANES), i32),
            pltpu.VMEM((lines, LANES), i32),
            pltpu.VMEM((send.shape[1], 1, LANES), i32),
            dma((8,)),
            pltpu.VMEM((2 * days, gauges), jnp.bfloat16),
            pltpu.VMEM((1, gauges), i32),
            pltpu.VMEM((levels, days) + tile, f32),
            pltpu.VMEM((days,) + tile, f32),
            pltpu.VMEM((levels, LAGS) + tile, f32),
            pltpu.VMEM((levels,) + tile, i32),
            pltpu.VMEM((levels,) + tile, i32),
            pltpu.VMEM((levels,) + tile, i32),
            pltpu.VMEM((rounds,) + tile, i32),
            pltpu.VMEM((rounds,) + tile, i32),
            pltpu.VMEM((levels,) + tile, f32),
            pltpu.VMEM((days + HALO,) + tile, f32),
            pltpu.VMEM((days,) + tile, f32),
            pltpu.VMEM((levels, days) + tile, f32),
            pltpu.VMEM((levels, HALO) + tile, f32),
            pltpu.VMEM((rounds, parts, 1, LANES), f32),
            pltpu.VMEM((rounds, parts, 1, LANES), f32),
            pltpu.VMEM((rounds, parts, 1, LANES), f32),
            pltpu.VMEM((2, LANES, LANES), f32),
            pltpu.VMEM((days, LANES), f32),
            pltpu.VMEM((days, LANES), f32),
            pltpu.VMEM((LAGS,) + tile, f32),
            pltpu.VMEM((levels, TILES, 2, 1, LANES), f32),
            pltpu.VMEM((rounds, shifts - 1, 2, 1, LANES), f32),
            pltpu.VMEM((shifts - 1, TILES, 2, 1, LANES), f32),
            pltpu.VMEM((rounds, 2, 1, LANES), f32),
            pltpu.VMEM((shifts, rounds, 2, 1, LANES), f32),
            pltpu.VMEM((2, levels * TILES, LANES), f32),
            pltpu.VMEM((levels * TILES, days, LANES), f32),
            pltpu.VMEM((lines, days, LANES), f32),
            dma((levels,)),
            dma((levels,)),
            dma((rounds,)),
            dma((rounds,)),
            dma((rounds,)),
            dma((rounds,)),
            dma((levels + 1,)),
            dma((levels + 1,)),
        ],
        compiler_params=pltpu.CompilerParams(
            collective_id=0, has_side_effects=True, vmem_limit_bytes=66000000
        ),
    )(
        block_level,
        cotangent,
        gauge_reach.reshape(1, gauges),
        inflow,
        shape_param.reshape(lines, LANES),
        scale_param.reshape(lines, LANES),
        down_local.reshape(lines, LANES),
        in_slot.reshape(lines, LANES),
        jnp.transpose(send, (1, 0, 2)),
    )


def solution(mesh):
    in_specs = (
        P("tm", "basin"),
        P("tm", "basin"),
        P("basin"),
        P("basin"),
        P("basin"),
        P("basin"),
        P("basin"),
        P("basin"),
        P("basin", None, None),
    )
    out_specs = (P("tm", "basin"), P(None, "basin"))
    body = functools.partial(shards, mesh.shape["basin"], mesh.shape["tm"])
    return jax.shard_map(body, mesh=mesh, in_specs=in_specs, out_specs=out_specs, check_vma=False)
```

```python
import functools
import math

import jax
import jax.numpy as jnp
from jax import lax
from jax.experimental import pallas as pl
from jax.experimental.pallas import tpu as pltpu
from jax.sharding import PartitionSpec as P

BLK = 256
LAGS = 30
LEVELS = 8
MAXB = 4
CAP = 4
LANES = 128
TILES = MAXB * BLK // LANES
HALO = LAGS - 1
OFFSETS = [k + 0.5 for k in range(LAGS)]
LOGS = [math.log(o) for o in OFFSETS]


def adjoint_kernel(
    parts,
    shifts,
    days,
    levels,
    cot_h,
    gauge_h,
    inflow_h,
    shape_h,
    scale_h,
    down_h,
    inslot_h,
    send_h,
    lat,
    par,
    table,
    cot,
    gauge,
    shape_p,
    scale_p,
    down,
    inslot,
    send,
    load_sem,
    cot2,
    gpos,
    seed,
    infl,
    kern,
    dlane,
    dtile,
    rlane,
    wlane,
    wtile,
    scl_lv,
    adj,
    lday,
    xsend,
    xrecv,
    out_msg,
    own_msg,
    far_msg,
    turn,
    rows_own,
    rows_far,
    lag_sum,
    psend,
    precv,
    plast,
    gsum,
    gall,
    ptotal,
    lat_lv,
    staged,
    sx,
    rx,
    so,
    sf,
    ro,
    rf,
    sp,
    rp,
):
    blocks = levels.shape[0]
    me = lax.axis_index("basin")
    shift = lax.axis_index("tm")
    prev = lax.rem(shift + shifts - 1, shifts)
    has_next = shift < shifts - 1
    has_prev = shift > 0
    side = max(1, math.isqrt(parts // 2))
    hops = [min(d, side - d) for d in range(side)]
    routes = [(y, x, c) for y in range(side) for x in range(side) for c in range(2)][1:]
    routes.sort(key=lambda r: -(hops[r[0]] + hops[r[1]]))

    def partner(route):
        y = lax.rem(me // (2 * side) + route[0], side)
        x = lax.rem(lax.rem(me // 2, side) + route[1], side)
        return (y * side + x) * 2 + lax.rem(me + route[2], 2)


    partners = [partner(route) for route in routes]

    def tile_of(reach):
        block = reach >> 8
        slot = jnp.zeros_like(reach)
        for b in range(blocks):
            slot = jnp.where(block == b, table[LEVELS * MAXB + b], slot)
        return slot, (slot & (MAXB - 1)) * 2 + ((reach >> 7) & 1)

    def prepare(h):
        spots = [table[h * MAXB + m] * 2 + j for m in range(MAXB) for j in range(2)]

        def tiled(ref):
            return jnp.concatenate([ref[pl.ds(i, 1), :] for i in spots], axis=0)

        target = tiled(down)
        dtile[h] = jnp.where(target >= 0, tile_of(target)[1], -1)
        dlane[h] = target & (LANES - 1)
        rlane[h] = tiled(inslot)
        shp = tiled(shape_p) - 1.0
        scl = tiled(scale_p)
        scl_lv[h] = scl
        weights = [jnp.exp(shp * LOGS[k] - OFFSETS[k] / scl) for k in range(LAGS)]
        total = weights[0]
        for k in range(1, LAGS):
            total = total + weights[k]
        for k in range(LAGS):
            kern[h, k] = weights[k] / total

    def seeds(h):
        width = 2 * LANES
        local = gpos[...] - h * (MAXB * BLK)

        ids = lax.broadcasted_iota(jnp.int32, (width, local.shape[1]), 0)
        for c in range(MAXB * BLK // width):
            hot = jnp.where(ids == local - c * width, 1.0, 0.0).astype(jnp.bfloat16)
            both = lax.dot_general(
                cot2[...], hot, (((1,), (1,)), ((), ())), preferred_element_type=jnp.float32
            )
            sums = both[:days] + both[days:]
            for j in range(width // LANES):
                seed[h, :, 2 * c + j, :] = sums[:, j * LANES : (j + 1) * LANES]

    def routed_own(h):
        for g in range(0, days, 8):
            total = kern[h, 0][None] * adj[pl.ds(g, 8)]
            for k in range(1, min(LAGS, days - 7 - g)):
                total = total + kern[h, k][None] * adj[pl.ds(g + k, 8)]
            lday[pl.ds(g, 8)] = total

    def routed_far(h):
        for g in range(0, days, 8):
            total = lday[pl.ds(g, 8)]
            for k in range(days - 7 - g, LAGS):
                total = total + kern[h, k][None] * adj[pl.ds(g + k, 8)]
            lday[pl.ds(g, 8)] = total

    def outgoing(h):
        lane, tile = wlane[h], wtile[h]
        for g in range(days // 8):
            picked = jnp.zeros((8, LANES), jnp.float32)
            for s in range(TILES):
                got = jnp.take_along_axis(lday[pl.ds(8 * g, 8), s, :], lane, axis=1)
                picked = jnp.where(tile == s, got, picked)
            turn[0, 8 * g : 8 * g + 8, :] = picked
        turn[0] = jnp.transpose(turn[0])
        lanes = lax.broadcasted_iota(jnp.int32, (parts, LANES), 1)
        packed = jnp.zeros((parts, LANES), jnp.float32)
        for c in range(CAP):
            piece = turn[0, pl.ds(c, parts, stride=CAP), :]
            piece = pltpu.roll(piece, c * days, axis=1) if c else piece
            packed = jnp.where((lanes >= c * days) & (lanes < (c + 1) * days), piece, packed)
        out_msg[h, :, 0, :] = packed

    def slot_copy(h, q, target, ssem, buf, rsem):
        return pltpu.make_async_remote_copy(
            src_ref=out_msg.at[h, q],
            dst_ref=buf.at[h, me],
            send_sem=ssem.at[h],
            recv_sem=rsem.at[h],
            device_id={"basin": q, "tm": target},
            device_id_type=pl.DeviceIdType.MESH,
        )

    def send_slots(h):
        @pl.when(has_prev)
        def _():
            for q in partners:
                slot_copy(h, q, prev, sf, far_msg, rf).start()
                slot_copy(h, q, shift, so, own_msg, ro).start()

        @pl.when(jnp.logical_not(has_prev))
        def _():
            for q in partners:
                slot_copy(h, q, shift, so, own_msg, ro).start()

    def local_part(h, first, count):
        lane, tile = dlane[h], dtile[h]
        masks = [tile == s for s in range(TILES)]
        for t in range(first, first + count):
            got = jnp.zeros((TILES, LANES), jnp.float32)
            for s in range(TILES):
                line = jnp.broadcast_to(lday[t, s : s + 1, :], (TILES, LANES))
                got = jnp.where(masks[s], jnp.take_along_axis(line, lane, axis=1), got)
            xsend[h, t] = seed[h, t] + got

    def halo_copy(h, first, count):
        return pltpu.make_async_remote_copy(
            src_ref=xsend.at[h, pl.ds(first, count)],
            dst_ref=xrecv.at[h, pl.ds(first, count)],
            send_sem=sx.at[h],
            recv_sem=rx.at[h],
            device_id={"basin": me, "tm": prev},
            device_id_type=pl.DeviceIdType.MESH,
        )

    def send_halo(h, first, count):
        @pl.when(has_prev)
        def _():
            halo_copy(h, first, count).start()

    def take_halo(h):
        @pl.when(has_next)
        def _():
            wait_bytes(xrecv.at[h], rx.at[h])

    def unpack(h, buf, rows):
        arrived = buf[h, :, 0, :]
        for c in range(CAP):
            piece = pltpu.roll(arrived, LANES - c * days, axis=1) if c else arrived
            turn[1, pl.ds(c, parts, stride=CAP), :] = piece
        rows[...] = jnp.transpose(turn[1])[: rows.shape[0]]

    def remote_part(h, row):
        slot = rlane[h]
        line = jnp.broadcast_to(row, (TILES, LANES))
        got = jnp.take_along_axis(line, slot & (LANES - 1), axis=1)
        return jnp.where(slot >= 0, got, 0.0)

    def gradient(h):
        for m in range(MAXB):
            block = table[h * MAXB + m]
            for j in range(2):
                infl[:, 2 * m + j, :] = staged[block * 2 + j]
        for k in range(LAGS):
            lag_sum[k] = jnp.sum(infl[...] * adj[pl.ds(k, days)], axis=0)
        mean = kern[h, 0] * lag_sum[0]
        for k in range(1, LAGS):
            mean = mean + kern[h, k] * lag_sum[k]
        first = jnp.zeros((TILES, LANES), jnp.float32)
        second = jnp.zeros((TILES, LANES), jnp.float32)
        for k in range(LAGS):
            logit = kern[h, k] * (lag_sum[k] - mean)
            first = first + logit * LOGS[k]
            second = second + logit * OFFSETS[k]
        scl = scl_lv[h]
        psend[h, :, 0, 0, :] = first
        psend[h, :, 1, 0, :] = second / (scl * scl)

    def peer_copy(src, dst, h, i):
        return pltpu.make_async_remote_copy(
            src_ref=src,
            dst_ref=dst,
            send_sem=sp.at[h],
            recv_sem=rp.at[h],
            device_id={"basin": me, "tm": lax.rem(shift + i, shifts)},
            device_id_type=pl.DeviceIdType.MESH,
        )

    def send_grads(h):
        for i in range(1, shifts):
            owner = lax.rem(shift + i, shifts)
            peer_copy(psend.at[h, owner], precv.at[h, i - 1], h, i).start()

    def keep(h):
        for s in range(TILES):
            lat_lv[h * TILES + s] = lday[:, s, :]

    def wait_bytes(ref, sem):
        pltpu.make_async_copy(ref, ref, sem).wait()

    barrier = pltpu.get_barrier_semaphore()

    def greet(q, k):
        where = {"basin": q, "tm": k}
        pl.semaphore_signal(barrier, inc=1, device_id=where, device_id_type=pl.DeviceIdType.MESH)

    loads = [
        pltpu.make_async_copy(src, dst, load_sem.at[i])
        for i, (src, dst) in enumerate(
            [(cot_h, cot), (gauge_h, gauge), (shape_h, shape_p), (scale_h, scale_p), (down_h, down), (inslot_h, inslot), (send_h, send)]
        )
    ]
    for copy in loads:
        copy.start()
    for i in range(2 * blocks):
        pltpu.make_async_copy(
            inflow_h.at[:, pl.ds(i * LANES, LANES)], staged.at[i], load_sem.at[len(loads)]
        ).start()

    everyone = partners + [me]

    @pl.when(has_prev)
    def _():
        for q in everyone:
            greet(q, prev)

    @pl.when(has_next)
    def _():
        for q in everyone:
            greet(q, shift + 1)

    for q in partners:
        greet(q, shift)
    for i in range(1, shifts):
        greet(me, lax.rem(shift + i, shifts))

    level_of = [levels[b] for b in range(blocks)]
    places = []
    for b in range(blocks):
        place = level_of[b] * MAXB
        for a in range(b):
            place = place + jnp.where(level_of[a] == level_of[b], 1, 0)
        places.append(place)
        table[LEVELS * MAXB + b] = place

    loads[0].wait()
    loads[1].wait()
    value = cot[...]
    high = value.astype(jnp.bfloat16)
    cot2[pl.ds(0, days), :] = high
    cot2[pl.ds(days, days), :] = (value - high.astype(jnp.float32)).astype(jnp.bfloat16)
    reach = gauge[...]
    gpos[...] = tile_of(reach)[0] * BLK + (reach & (BLK - 1))

    @pl.when(shift == shifts - 1)
    def _():
        xrecv[0] = jnp.zeros_like(xrecv[0])
        adj[pl.ds(days, HALO)] = jnp.zeros((HALO, TILES, LANES), jnp.float32)

    seeds(0)
    xsend[0] = seed[0]
    greeted = parts - 1 + shifts - 1
    greeted = greeted + parts * (has_prev.astype(jnp.int32) + has_next.astype(jnp.int32))
    pl.semaphore_wait(barrier, greeted)
    send_halo(0, 0, HALO)

    @pl.loop(0, LEVELS * MAXB)
    def _(i):
        block = jnp.int32(0)
        for b in range(1, blocks):
            block = block + jnp.where(places[b] == i, b, 0)
        table[i] = block

    for copy in loads[2:]:
        copy.wait()
    for h in range(LEVELS - 1):
        wanted = jnp.broadcast_to(jnp.maximum(send[h], 0), (8, LANES))
        wlane[h] = wanted & (LANES - 1)
        wtile[h] = tile_of(wanted)[1]
    turn[...] = jnp.zeros_like(turn)
    pltpu.make_async_copy(staged, staged, load_sem.at[len(loads)]).wait()
    prepare(0)
    prepare(1)
    seeds(1)
    adj[pl.ds(0, days)] = xsend[0]
    routed_own(0)
    take_halo(0)
    adj[pl.ds(days, HALO)] = xrecv[0]

    @pl.loop(0, LEVELS - 1)
    def _(h):
        routed_far(h)
        outgoing(h)
        send_slots(h)
        half = days // 2
        local_part(h + 1, 0, half)
        send_halo(h + 1, 0, half)
        local_part(h + 1, half, days - half)
        send_halo(h + 1, half, HALO - half)
        gradient(h)
        keep(h)

        @pl.when(h < LEVELS - 2)
        def _():
            seeds(h + 2)

        prepare(jnp.minimum(h + 2, LEVELS - 1))
        send_grads(h)
        wait_bytes(own_msg.at[h, pl.ds(0, parts - 1)], ro.at[h])
        unpack(h, own_msg, rows_own)
        for t in range(days):
            adj[t] = xsend[h + 1, t] + remote_part(h + 1, rows_own[t : t + 1, :])
        routed_own(h + 1)

        @pl.when(has_next)
        def _():
            wait_bytes(far_msg.at[h, pl.ds(0, parts - 1)], rf.at[h])
            unpack(h, far_msg, rows_far)
            take_halo(h + 1)
            for t in range(HALO):
                adj[days + t] = xrecv[h + 1, t] + remote_part(h + 1, rows_far[t : t + 1, :])

    last = LEVELS - 1
    gradient(last)
    for i in range(1, shifts):
        peer_copy(psend.at[last], plast.at[i - 1], last, i).start()

    @pl.loop(0, last)
    def _(h):
        wait_bytes(precv.at[h], rp.at[h])
        total = psend[h, shift]
        for i in range(shifts - 1):
            total = total + precv[h, i]
        gsum[h] = total

    for i in range(1, shifts):
        peer_copy(gsum, gall.at[shift], LEVELS, i).start()
    gall[shift] = gsum[...]
    routed_far(last)
    keep(last)
    for b in range(blocks):
        place = table[LEVELS * MAXB + b]
        for j in range(2):
            lat[:, pl.ds(b * BLK + j * LANES, LANES)] = lat_lv[place * 2 + j]
    wait_bytes(gall.at[pl.ds(0, shifts - 1)], rp.at[LEVELS])
    for h in range(last):
        for r in range(2):
            ptotal[r, h * TILES : (h + 1) * TILES, :] = gall[:, h, r, 0, :]
    wait_bytes(plast, rp.at[last])
    for r in range(2):
        total = psend[last, :, r, 0, :]
        for i in range(shifts - 1):
            total = total + plast[i, :, r, 0, :]
        ptotal[r, last * TILES : LEVELS * TILES, :] = total

    for b in range(blocks):
        place = table[LEVELS * MAXB + b]
        for j in range(2):
            for r in range(2):
                line = ptotal[r, pl.ds(place * 2 + j, 1), :]
                par[r : r + 1, pl.ds(b * BLK + j * LANES, LANES)] = line

    @pl.loop(0, LEVELS)
    def _(h):

        @pl.when(has_prev)
        def _():
            wait_bytes(xsend.at[h, pl.ds(0, HALO)], sx.at[h])

    @pl.loop(0, LEVELS - 1)
    def _(h):
        wait_bytes(out_msg.at[h, pl.ds(0, parts - 1)], so.at[h])
        wait_bytes(precv.at[h], sp.at[h])

        @pl.when(has_prev)
        def _():
            wait_bytes(out_msg.at[h, pl.ds(0, parts - 1)], sf.at[h])
    wait_bytes(plast, sp.at[last])
    wait_bytes(gall.at[pl.ds(0, shifts - 1)], sp.at[LEVELS])


def shards(parts, shifts, inflow, cotangent, gauge_reach, shape_param, scale_param, block_level, down_local, in_slot, send_reach):
    days, reaches = inflow.shape
    gauges = cotangent.shape[1]
    lines = reaches // LANES
    send = send_reach
    if send.shape[2] < LANES:
        send = jnp.pad(send, ((0, 0), (0, 0), (0, LANES - send.shape[2])))
    f32, i32 = jnp.float32, jnp.int32
    levels = LEVELS
    rounds = LEVELS - 1
    tile = (TILES, LANES)
    vmem = pl.BlockSpec(memory_space=pltpu.VMEM)
    hbm = pl.BlockSpec(memory_space=pltpu.HBM)
    dma = pltpu.SemaphoreType.DMA
    return pl.pallas_call(
        functools.partial(adjoint_kernel, parts, shifts, days),
        out_shape=(
            jax.ShapeDtypeStruct((days, reaches), f32),
            jax.ShapeDtypeStruct((2, reaches), f32),
        ),
        in_specs=[pl.BlockSpec(memory_space=pltpu.SMEM)] + [hbm] * 8,
        out_specs=(vmem, vmem),
        scratch_shapes=[
            pltpu.SMEM((LEVELS * MAXB + block_level.shape[0],), i32),
            pltpu.VMEM((days, gauges), f32),
            pltpu.VMEM((1, gauges), i32),
            pltpu.VMEM((lines, LANES), f32),
            pltpu.VMEM((lines, LANES), f32),
            pltpu.VMEM((lines, LANES), i32),
            pltpu.VMEM((lines, LANES), i32),
            pltpu.VMEM((send.shape[1], 1, LANES), i32),
            dma((8,)),
            pltpu.VMEM((2 * days, gauges), jnp.bfloat16),
            pltpu.VMEM((1, gauges), i32),
            pltpu.VMEM((levels, days) + tile, f32),
            pltpu.VMEM((days,) + tile, f32),
            pltpu.VMEM((levels, LAGS) + tile, f32),
            pltpu.VMEM((levels,) + tile, i32),
            pltpu.VMEM((levels,) + tile, i32),
            pltpu.VMEM((levels,) + tile, i32),
            pltpu.VMEM((rounds,) + tile, i32),
            pltpu.VMEM((rounds,) + tile, i32),
            pltpu.VMEM((levels,) + tile, f32),
            pltpu.VMEM((days + HALO,) + tile, f32),
            pltpu.VMEM((days,) + tile, f32),
            pltpu.VMEM((levels, days) + tile, f32),
            pltpu.VMEM((levels, HALO) + tile, f32),
            pltpu.VMEM((rounds, parts, 1, LANES), f32),
            pltpu.VMEM((rounds, parts, 1, LANES), f32),
            pltpu.VMEM((rounds, parts, 1, LANES), f32),
            pltpu.VMEM((2, LANES, LANES), f32),
            pltpu.VMEM((days, LANES), f32),
            pltpu.VMEM((days, LANES), f32),
            pltpu.VMEM((LAGS,) + tile, f32),
            pltpu.VMEM((levels, TILES, 2, 1, LANES), f32),
            pltpu.VMEM((rounds, shifts - 1, 2, 1, LANES), f32),
            pltpu.VMEM((shifts - 1, TILES, 2, 1, LANES), f32),
            pltpu.VMEM((rounds, 2, 1, LANES), f32),
            pltpu.VMEM((shifts, rounds, 2, 1, LANES), f32),
            pltpu.VMEM((2, levels * TILES, LANES), f32),
            pltpu.VMEM((levels * TILES, days, LANES), f32),
            pltpu.VMEM((lines, days, LANES), f32),
            dma((levels,)),
            dma((levels,)),
            dma((rounds,)),
            dma((rounds,)),
            dma((rounds,)),
            dma((rounds,)),
            dma((levels + 1,)),
            dma((levels + 1,)),
        ],
        compiler_params=pltpu.CompilerParams(
            collective_id=0, has_side_effects=True, vmem_limit_bytes=66000000
        ),
    )(
        block_level,
        cotangent,
        gauge_reach.reshape(1, gauges),
        inflow,
        shape_param.reshape(lines, LANES),
        scale_param.reshape(lines, LANES),
        down_local.reshape(lines, LANES),
        in_slot.reshape(lines, LANES),
        jnp.transpose(send, (1, 0, 2)),
    )


def solution(mesh):
    in_specs = (
        P("tm", "basin"),
        P("tm", "basin"),
        P("basin"),
        P("basin"),
        P("basin"),
        P("basin"),
        P("basin"),
        P("basin"),
        P("basin", None, None),
    )
    out_specs = (P("tm", "basin"), P(None, "basin"))
    body = functools.partial(shards, mesh.shape["basin"], mesh.shape["tm"])
    return jax.shard_map(body, mesh=mesh, in_specs=in_specs, out_specs=out_specs, check_vma=False)
```
